32 devices in a mesh: blk: 8 (over z, y), pix: 4 (over x, core).
Axes of the slice: x: 2, y: 2, z: 4, core: 2. Of those that a mesh axis runs over, the one named last changes fastest.
Arguments:
- images: bfloat16 [256, 16384], P('blk', 'pix'), may hold values from -14 to 14
- templates: bfloat16 [2304, 16384], P('blk', 'pix'), may hold values from -4 to 4
- routes: int32 [256, 4], P('blk'), may hold values from 0 to 7, all different within a row; in each aligned block of 32 rows (0 to 31, 32 to 63, ...) at most 24 rows name the same one
- image_weight: float32 [256], P('blk'), may hold values from 0.25 to 4
- template_weight: float32 [2304], P('blk'), may hold values from 0.25 to 4
Outputs:
- template_means: bfloat16 [2304, 16384], P('blk', 'pix')
- image_duals: float32 [256], P('blk')
The draws below stay inside these ranges and needn't reach their ends.
Inputs may be any that keep to these rules, and one draw needn't show every extreme that they name: `routes`: each image names 4 different template blocks. Among the 32 images of one block, at most 24 name any one template block, and some template block is named by exactly 24 of them. Every template block is named by some image.
All inputs are finite; a program needn't handle non-finite values.
Results may differ from the reference program's by a relative error of at most 0.0046.
Values may be sent and summed in bfloat16 or wider, within the bound.
A program may use at most 64 MiB of HBM per device.

```python
import math
import jax
import jax.numpy as jnp
import numpy as np
from jax import lax

PIX = 16384
IMG_DEV = 32
TPL_DEV = 288
TOP = 4
SWEEPS = 2
NI = 256
NT = 2304
MOST = 24
N_BLK = 8


def draw_images(key, part):
    spread = jnp.exp(jax.random.uniform(jax.random.fold_in(key, 17), (NI, 1), jnp.float32, math.log(0.3), math.log(3.0)))
    values = spread * jax.random.truncated_normal(jax.random.fold_in(key, 19), -4.0, 4.0, (NI, PIX), jnp.float32)
    return values.astype(jnp.bfloat16)


def draw_templates(key, part):
    spread = jnp.exp(jax.random.uniform(jax.random.fold_in(key, 23), (NT, 1), jnp.float32, math.log(0.5), math.log(2.0)))
    values = spread * jax.random.truncated_normal(jax.random.fold_in(key, 29), -4.0, 4.0, (NT, PIX), jnp.float32) / math.sqrt(PIX)
    return values.astype(jnp.bfloat16)


def block_levels(stream_key, extent, cuts, low, high):
    gain = 1.0
    for dim, parts in cuts:
        steps = jax.random.uniform(jax.random.fold_in(jax.random.fold_in(stream_key, 6), dim), (parts,), jnp.float32, low / len(cuts), high / len(cuts))
        gain = gain * jnp.repeat(jnp.exp(steps), extent[dim] // parts).reshape((-1,) + (1,) * (len(extent) - 1 - dim))
    return gain


def assign_block(own_key, own, number, rows, number_of, top, limit, skew):
    ranking = jax.random.permutation(own_key, number_of)
    packed, ordinary = portions_of(number_of, rows * top, limit, skew, True), portions_of(number_of, rows * top, limit, skew, False)
    places = jnp.arange(number_of)

    def named(lengths, offset_by):
        used = int((lengths > 0).sum())
        fixed = max(1, used // 4)
        moved = fixed + (places - fixed + offset_by * (used - fixed)) % max(1, number_of - fixed)
        return jnp.zeros((number_of,), jnp.int32).at[ranking[jnp.where(places < fixed, places, moved)]].set(jnp.asarray(lengths, jnp.int32))

    lengths = jnp.where(number % 4 == 0, named(packed, number // 4), named(ordinary, number - number // 4 - 1))
    mixed = jax.random.permutation(jax.random.fold_in(own, 3), number_of)
    source_of, taker = mixed[0:number_of // 2 * 2:2], mixed[1:number_of // 2 * 2:2]
    room = jnp.minimum(lengths[source_of] - 1, limit - lengths[taker]) // 2
    room = jnp.where((source_of == ranking[0]) | (taker == ranking[0]) | (lengths[taker] == 0), 0, jnp.maximum(room, 0))
    moved = jax.random.randint(jax.random.fold_in(own, 4), (number_of // 2,), 0, 1 << 20) % (room + 1)
    lengths = lengths.at[source_of].add(-moved).at[taker].add(moved)
    items = jnp.searchsorted(jnp.cumsum(lengths), jnp.arange(rows * top), side="right").astype(jnp.int32)
    table = items.reshape(top, rows).T
    table = table[jax.random.permutation(jax.random.fold_in(own, 1), rows)]
    offset_by = jax.random.randint(jax.random.fold_in(own, 2), (rows, 1), 0, top)
    return jnp.take_along_axis(table, (jnp.arange(top)[None, :] + offset_by) % top, axis=1)


def portions_of(number_of, total, reach, lean, full):
    weights = [(1 << 20) // math.isqrt(standing ** lean) + 1 for standing in range(1, number_of + 1)]
    largest = reach if full else min(reach, max(-(-total // number_of), total * weights[0] // sum(weights)))
    least = 1 if total - largest >= number_of - 1 else 0
    counts, surplus = [largest] + [least] * (number_of - 1), total - largest - least * (number_of - 1)
    while surplus > 0:
        movable = [i for i in range(1, number_of) if counts[i] < largest] or [i for i in range(1, number_of) if counts[i] < reach]
        pool, budget = sum([weights[i] for i in movable]), surplus
        for i in movable:
            addition = min(reach - counts[i], max(1, budget * weights[i] // pool), surplus)
            counts[i] = counts[i] + addition
            surplus = surplus - addition
    return np.array(counts)


def setup_inputs(seed: int = 0) -> dict:
    key_of = jax.random.split(jax.random.key(seed), 6)
    images = draw_images(jax.random.fold_in(key_of[5], 71), 0)
    templates = draw_templates(jax.random.fold_in(key_of[5], 71), 0)
    routes_keys = jax.random.split(jax.random.fold_in(key_of[2], 1), NI // IMG_DEV)
    routes_turns = jax.random.permutation(jax.random.fold_in(key_of[2], 3), NI // IMG_DEV)
    routes = jax.vmap(lambda own, number: assign_block(jax.random.fold_in(key_of[2], 2), own, number, IMG_DEV, N_BLK, TOP, MOST, 2))(routes_keys, routes_turns).reshape((NI, TOP))
    image_weight = jnp.clip(jnp.exp(math.log(4.0) - 2.7725887 * jax.random.uniform(key_of[3], (NI,), jnp.float32) ** block_levels(key_of[3], (NI,), ((0, 8),), -0.2, 0.2)), 0.25, 4.0)
    template_weight = jnp.clip(jnp.exp(math.log(4.0) - 2.7725887 * jax.random.uniform(key_of[4], (NT,), jnp.float32) ** block_levels(key_of[4], (NT,), ((0, 8),), -0.2, 0.2)), 0.25, 4.0)
    return dict(images=images, templates=templates, routes=routes, image_weight=image_weight, template_weight=template_weight)


def route_positions(routes):
    target = routes.reshape(N_BLK, IMG_DEV * TOP)

    def one_block(target_row):
        target_hot = (target_row[:, None] == jnp.arange(N_BLK, dtype=jnp.int32)[None, :]).astype(jnp.int32)
        before = jnp.cumsum(target_hot, axis=0) - target_hot
        return jnp.sum(before * target_hot, axis=1).astype(jnp.int32)

    position = lax.map(one_block, target)
    return target, position


def reference(images, templates, routes, image_weight, template_weight):
    target, position = route_positions(routes)
    source_slot = jnp.arange(N_BLK, dtype=jnp.int32)[:, None] * MOST + position
    image_index = (jnp.arange(NI * TOP, dtype=jnp.int32) // TOP).reshape(N_BLK, IMG_DEV * TOP)
    table = jnp.full((N_BLK, N_BLK * MOST), -1, jnp.int32).at[target, source_slot].set(image_index)
    usable = table >= 0
    safe_index = jnp.maximum(table, 0).astype(jnp.int32)
    template_blocks = templates.reshape(N_BLK, TPL_DEV, PIX)

    def score_block(pieces):
        index_row, block = pieces
        rows = images[index_row]
        return jnp.dot(rows, block.T, preferred_element_type=jnp.float32)

    scores = lax.map(score_block, (safe_index, template_blocks))
    image_log = jnp.log(image_weight)
    template_log = jnp.log(template_weight).reshape(N_BLK, TPL_DEV)
    image_duals = jnp.zeros((NI,), jnp.float32)
    for sweep_index in range(SWEEPS):
        slot_duals = jnp.where(usable, image_duals[safe_index], 0.0)
        column_terms = jnp.where(usable[:, :, None], scores + slot_duals[:, :, None], -jnp.inf)
        column_peak = jnp.max(column_terms, axis=1)
        template_duals = template_log - column_peak - jnp.log(jnp.sum(jnp.exp(column_terms - column_peak[:, None, :]), axis=1))
        row_terms = scores + template_duals[:, None, :]
        row_peak = jnp.max(row_terms, axis=2)
        row_total = jnp.sum(jnp.exp(row_terms - row_peak[:, :, None]), axis=2)
        peak_routes = row_peak[target, source_slot].reshape(NI, TOP)
        total_routes = row_total[target, source_slot].reshape(NI, TOP)
        route_peak = jnp.max(peak_routes, axis=1)
        image_duals = image_log - route_peak - jnp.log(jnp.sum(total_routes * jnp.exp(peak_routes - route_peak[:, None]), axis=1))
    slot_duals = jnp.where(usable, image_duals[safe_index], 0.0)
    column_terms = jnp.where(usable[:, :, None], scores + slot_duals[:, :, None], -jnp.inf)
    column_peak = jnp.max(column_terms, axis=1)
    column_exp = jnp.exp(column_terms - column_peak[:, None, :])
    plan_weights = (column_exp / jnp.sum(column_exp, axis=1, keepdims=True)).astype(jnp.bfloat16)

    def mean_block(pieces):
        index_row, weights_block = pieces
        rows = images[index_row]
        return jnp.dot(weights_block.T, rows, preferred_element_type=jnp.float32).astype(jnp.bfloat16)

    template_means = lax.map(mean_block, (safe_index, plan_weights)).reshape(NT, PIX)
    return template_means, image_duals
```

```python
import functools
import jax
import jax.numpy as jnp
from jax import lax
from jax.experimental import pallas as pl
from jax.experimental.pallas import tpu as pltpu
from jax.sharding import PartitionSpec as P

SWEEPS = 2
LINES = 2
CHUNKS = 8
LAG = 2
NEG = -1e30
MESH = pl.DeviceIdType.MESH
UP, DOWN, ACROSS = 0, 1, 2


def routed(images, templates, routes, image_weight, template_weight):
    blocks = lax.axis_size("blk")
    img_dev = images.shape[0]
    admits = routes.shape[1]
    capacity = max(2, (3 * img_dev * admits + 2 * blocks - 1) // (2 * blocks))
    target = routes.reshape(-1)
    target_hot = (target[:, None] == jnp.arange(blocks, dtype=jnp.int32)[None, :]).astype(jnp.int32)
    before = jnp.cumsum(target_hot, axis=0) - target_hot
    position = jnp.sum(before * target_hot, axis=1)
    slot_of = target * capacity + position
    wanted = jnp.arange(blocks * capacity, dtype=jnp.int32)
    matches = slot_of[None, :] == wanted[:, None]
    filled = jnp.any(matches, axis=1)
    owner_image = jnp.sum(
        jnp.where(matches, jnp.arange(target.shape[0], dtype=jnp.int32)[None, :] // admits, 0),
        axis=1,
    )
    outgoing = jnp.where(filled[:, None], images[owner_image], jnp.zeros((), images.dtype))
    outgoing = outgoing.reshape(blocks, capacity, images.shape[1])
    slot_flags = filled.astype(jnp.bfloat16).reshape(blocks, capacity)
    template_log = jnp.log(template_weight)
    arrived_piece = lax.all_to_all(outgoing, "blk", split_axis=0, concat_axis=0, tiled=True)
    marks_piece = lax.all_to_all(slot_flags, "blk", split_axis=0, concat_axis=0, tiled=True)
    partial_value = jnp.einsum(
        "bmp,tp->bmt", arrived_piece, templates, preferred_element_type=jnp.float32
    )
    summed = lax.psum(partial_value, "pix")
    usable = marks_piece > 0
    image_log = jnp.log(image_weight)
    slot_duals = jnp.zeros((blocks, capacity), jnp.float32)
    image_duals = jnp.zeros((img_dev,), jnp.float32)
    for sweep_index in range(SWEEPS):
        column_terms = jnp.where(usable[:, :, None], summed + slot_duals[:, :, None], -jnp.inf)
        column_peak = jnp.max(column_terms, axis=(0, 1))
        template_duals = (
            template_log
            - column_peak
            - jnp.log(jnp.sum(jnp.exp(column_terms - column_peak), axis=(0, 1)))
        )
        row_terms = summed + template_duals
        row_peak = jnp.max(row_terms, axis=2)
        row_total = jnp.sum(jnp.exp(row_terms - row_peak[:, :, None]), axis=2)
        levels = row_peak + jnp.log(row_total)
        back_levels = lax.all_to_all(levels, "blk", split_axis=0, concat_axis=0, tiled=True)
        level_routes = back_levels.reshape(-1)[slot_of].reshape(img_dev, admits)
        route_peak = jnp.max(level_routes, axis=1)
        image_duals = (
            image_log
            - route_peak
            - jnp.log(jnp.sum(jnp.exp(level_routes - route_peak[:, None]), axis=1))
        )
        duals_send = jnp.where(filled, image_duals[owner_image], 0.0).reshape(blocks, capacity)
        slot_duals = lax.all_to_all(duals_send, "blk", split_axis=0, concat_axis=0, tiled=True)
    column_terms = jnp.where(usable[:, :, None], summed + slot_duals[:, :, None], -jnp.inf)
    column_peak = jnp.max(column_terms, axis=(0, 1))
    column_exp = jnp.exp(column_terms - column_peak)
    plan_weights = (column_exp / jnp.sum(column_exp, axis=(0, 1))).astype(jnp.bfloat16)
    template_means = jnp.einsum(
        "bmt,bmp->tp", plan_weights, arrived_piece, preferred_element_type=jnp.float32
    ).astype(jnp.bfloat16)
    return (template_means, image_duals)


def gather_and_plan(dims, img_hbm, tpl_hbm, info_ref, tlog_ref, gath_hbm, plan_ref, dual_ref,
                    buf, infos, tpl, acc, parts, lse_out, lse_in,
                    send_sem, recv_sem, info_send, info_recv, local_sem,
                    part_send, part_recv, lse_send, lse_recv, plan_send, plan_recv):
    blocks, pixes, admits, tpl_dev, share = dims
    depth = blocks // LINES
    rows, pixels = img_hbm.shape
    width = pixels // CHUNKS
    b, p = lax.axis_index("blk"), lax.axis_index("pix")
    z, y = b // LINES, b % LINES
    other = 1 - y
    has_up, has_down = z < depth - 1, z > 0
    target = {UP: b + LINES, DOWN: b - LINES, ACROSS: z * LINES + other}
    allowed = {UP: has_up, DOWN: has_down}

    tpl_copy = pltpu.make_async_copy(tpl_hbm, tpl, local_sem.at[0])
    own_copy = pltpu.make_async_copy(img_hbm, buf.at[b], local_sem.at[1])
    info_copy = pltpu.make_async_copy(info_ref, infos.at[b], local_sem.at[2])
    tpl_copy.start()
    own_copy.start()
    info_copy.start()

    barrier = pltpu.get_barrier_semaphore()
    for way in (UP, DOWN):
        @pl.when(allowed[way])
        def _():
            pl.semaphore_signal(barrier, inc=1, device_id={"blk": target[way]}, device_id_type=MESH)
    pl.semaphore_signal(barrier, inc=1, device_id={"blk": target[ACROSS]}, device_id_type=MESH)
    for j in range(1, pixes):
        pl.semaphore_signal(barrier, inc=1, device_id={"pix": lax.rem(p + j, pixes)}, device_id_type=MESH)
    near = jnp.where(has_up, 1, 0) + jnp.where(has_down, 1, 0) + pixes
    pl.semaphore_wait(barrier, near)

    def cols(c):
        return pl.ds(c * width, width)

    def piece(way, k, c, own=False):
        return pltpu.make_async_remote_copy(
            src_ref=img_hbm.at[:, cols(c)] if own else buf.at[k, :, cols(c)],
            dst_ref=buf.at[k, :, cols(c)],
            send_sem=send_sem.at[way, k], recv_sem=recv_sem.at[k, c],
            device_id={"blk": target[way]}, device_id_type=MESH)

    def info_piece(way, k, own=False):
        return pltpu.make_async_remote_copy(
            src_ref=info_ref if own else infos.at[k], dst_ref=infos.at[k],
            send_sem=info_send.at[way, k], recv_sem=info_recv.at[k],
            device_id={"blk": target[way]}, device_id_type=MESH)

    def arrived(k, c):
        pltpu.make_async_copy(buf.at[k, :, cols(c)], buf.at[k, :, cols(c)], recv_sem.at[k, c]).wait()

    def info_arrived(k):
        pltpu.make_async_copy(infos.at[k], infos.at[k], info_recv.at[k]).wait()

    def along(way, start):
        @pl.when(allowed[way])
        def _():
            start()

    for c in range(CHUNKS):
        piece(ACROSS, b, c, True).start()
        for way in (UP, DOWN):
            along(way, lambda: piece(way, b, c, True).start())
    info_piece(ACROSS, b, True).start()
    for way in (UP, DOWN):
        along(way, lambda: info_piece(way, b, True).start())
    mate = z * LINES + other
    arrived(mate, 0)
    for way in (UP, DOWN):
        along(way, lambda: piece(way, mate, 0).start())

    def sides(d):
        return ((UP, z - d, z >= d), (DOWN, z + d, z + d < depth))

    def pass_on(d, c):
        for way, from_z, there in sides(d):
            k = from_z * LINES + y

            @pl.when(there)
            def _():
                arrived(k, c)
                if c:
                    piece(ACROSS, k, c).start()
                along(way, lambda: piece(way, k, c).start())

    def pass_rest(d):
        for way, from_z, there in sides(d):
            k, k2 = from_z * LINES + y, from_z * LINES + other

            @pl.when(there)
            def _():
                arrived(k2, 0)
                along(way, lambda: piece(way, k2, 0).start())
                info_arrived(k)
                info_piece(ACROSS, k).start()
                along(way, lambda: info_piece(way, k).start())

    def crossed(c):
        if c:
            arrived(mate, c)
            for d in range(1, depth):
                for way, from_z, there in sides(d):
                    @pl.when(there)
                    def _():
                        arrived(from_z * LINES + other, c)

    def product(c):
        images = buf[:, :, c * width:(c + 1) * width].reshape(blocks * rows, width)
        term = lax.dot_general(tpl[:, c * width:(c + 1) * width], images, (((1,), (1,)), ((), ())),
                               preferred_element_type=jnp.float32)
        if c == 1:
            acc[0:tpl_dev, :] = term
        else:
            acc[0:tpl_dev, :] += term

    for d in range(1, depth - 1):
        for c in range(CHUNKS):
            pass_on(d, c)
        pass_rest(d)
    own_copy.wait()
    tpl_copy.wait()
    if share * pixes > tpl_dev:
        acc[tpl_dev:, :] = jnp.zeros((share * pixes - tpl_dev, blocks * rows), jnp.float32)
    for c in range(CHUNKS + LAG):
        if c < CHUNKS:
            pass_on(depth - 1, c)
        if c == CHUNKS - 1:
            pass_rest(depth - 1)
        if c == CHUNKS + LAG - 1:
            product(0)
        if c > LAG:
            crossed(c - LAG)
            product(c - LAG)

    def my_part(j):
        return pltpu.make_async_remote_copy(
            src_ref=acc.at[pl.ds(lax.rem(p + j, pixes) * share, share), :], dst_ref=parts.at[j - 1],
            send_sem=part_send.at[j - 1], recv_sem=part_recv.at[j - 1],
            device_id={"pix": lax.rem(p + j, pixes)}, device_id_type=MESH)

    for j in range(1, pixes):
        my_part(j).start()
    back = pltpu.make_async_copy(buf, gath_hbm, local_sem.at[3])
    back.start()

    info_copy.wait()
    info_arrived(mate)
    for d in range(1, depth):
        for way, from_z, there in sides(d):
            @pl.when(there)
            def _():
                info_arrived(from_z * LINES + other)
    info = jnp.sum(infos[...], axis=0)
    code = (b + 1).astype(jnp.float32)
    admitted = jnp.max(jnp.where(info[0:admits, :] == code, 1.0, 0.0), axis=0, keepdims=True)
    image_log = info[admits:admits + 1, :]
    first = p * share
    template_log = tlog_ref[pl.ds(pl.multiple_of(first, 16), share), :]
    valid = first + lax.broadcasted_iota(jnp.int32, (share, 1), 0) < tpl_dev
    scores = acc[pl.ds(pl.multiple_of(first, 16), share), :]
    for j in range(1, pixes):
        my_part(j).wait_recv()
        scores = scores + parts[j - 1]
    scores = jnp.where(admitted > 0, scores, NEG)

    me = b * pixes + p
    devices = blocks * pixes
    duals = jnp.zeros((1, blocks * rows), jnp.float32)
    for sweep in range(SWEEPS):
        terms = scores + duals
        peak = jnp.max(terms, axis=1, keepdims=True)
        level = template_log - peak - jnp.log(jnp.sum(jnp.exp(terms - peak), axis=1, keepdims=True))
        level = jnp.where(valid, level, NEG)
        terms = scores + level
        peak = jnp.max(terms, axis=0, keepdims=True)
        lse = peak + jnp.log(jnp.sum(jnp.exp(terms - peak), axis=0, keepdims=True))
        lse_out[sweep] = lse

        def post(j, carry):
            to = lax.rem(me + j, devices)
            pltpu.make_async_remote_copy(
                src_ref=lse_out.at[sweep], dst_ref=lse_in.at[sweep, me],
                send_sem=lse_send.at[sweep], recv_sem=lse_recv.at[sweep],
                device_id={"blk": to // pixes, "pix": lax.rem(to, pixes)}, device_id_type=MESH).start()
            return carry

        lax.fori_loop(1, devices, post, 0)
        lse_in[sweep, me] = lse
        span = lse_in.at[sweep, pl.ds(0, devices - 1)]
        pltpu.make_async_copy(span, span, lse_recv.at[sweep]).wait()
        every = lse_in[sweep]
        peak = jnp.max(every, axis=0)
        duals = image_log - peak - jnp.log(jnp.sum(jnp.exp(every - peak), axis=0))
    dual_ref[...] = duals
    terms = scores + duals
    weight = jnp.exp(terms - jnp.max(terms, axis=1, keepdims=True))
    mine = pl.ds(pl.multiple_of(first, 16), share)
    plan_ref[mine, :] = (weight / jnp.sum(weight, axis=1, keepdims=True)).astype(jnp.bfloat16)

    def my_plan(j):
        return pltpu.make_async_remote_copy(
            src_ref=plan_ref.at[mine, :], dst_ref=plan_ref.at[mine, :],
            send_sem=plan_send.at[j - 1], recv_sem=plan_recv.at[j - 1],
            device_id={"pix": lax.rem(p + j, pixes)}, device_id_type=MESH)

    for j in range(1, pixes):
        my_plan(j).start()

    full = buf.at[b]
    rest = buf.at[b, :, pl.ds(width, pixels - width)]
    one = buf.at[b, :, pl.ds(0, width)]

    def left(ref, sem):
        pltpu.make_async_copy(ref, ref, sem).wait()

    left(full, send_sem.at[ACROSS, b])
    left(infos.at[b], info_send.at[ACROSS, b])
    for way in (UP, DOWN):
        along(way, lambda: (left(full, send_sem.at[way, b]), left(one, send_sem.at[way, mate]),
                            left(infos.at[b], info_send.at[way, b])) and None)
    for d in range(1, depth):
        for way, from_z, there in sides(d):
            k, k2 = from_z * LINES + y, from_z * LINES + other

            @pl.when(there)
            def _():
                left(rest, send_sem.at[ACROSS, k])
                left(infos.at[b], info_send.at[ACROSS, k])
                along(way, lambda: (left(full, send_sem.at[way, k]), left(one, send_sem.at[way, k2]),
                                    left(infos.at[b], info_send.at[way, k])) and None)
    for j in range(1, pixes):
        my_part(j).wait_send()
    for sweep in range(SWEEPS):
        span = lse_in.at[sweep, pl.ds(0, devices - 1)]
        left(span, lse_send.at[sweep])
    back.wait()
    for j in range(1, pixes):
        my_plan(j).wait_send()
        my_plan(j).wait_recv()


def gathered(images, templates, routes, image_weight, template_weight):
    blocks, pixes = lax.axis_size("blk"), lax.axis_size("pix")
    rows, pixels = images.shape
    tpl_dev, admits = templates.shape[0], routes.shape[1]
    share = -(-tpl_dev // (16 * pixes)) * 16
    b = lax.axis_index("blk")
    info = jnp.concatenate([routes.T.astype(jnp.float32) + 1.0, jnp.log(image_weight)[None, :]], axis=0)
    info = jnp.pad(info, ((0, -(admits + 1) % 8), (0, 0)))
    deep = info.shape[0]
    spot = jnp.arange(blocks * rows, dtype=jnp.int32)[None, :] // rows == b
    info = jnp.where(spot, jnp.tile(info, (1, blocks)), 0.0)
    tlog = jnp.pad(jnp.log(template_weight), (0, share * pixes - tpl_dev))[:, None]
    dims = (blocks, pixes, admits, tpl_dev, share)
    any_spec, vmem = pl.BlockSpec(memory_space=pl.ANY), pl.BlockSpec(memory_space=pltpu.VMEM)
    dma = pltpu.SemaphoreType.DMA
    devices = blocks * pixes
    gath, plan, duals = pl.pallas_call(
        functools.partial(gather_and_plan, dims),
        out_shape=(jax.ShapeDtypeStruct((blocks, rows, pixels), images.dtype),
                   jax.ShapeDtypeStruct((share * pixes, blocks * rows), jnp.bfloat16),
                   jax.ShapeDtypeStruct((1, blocks * rows), jnp.float32)),
        in_specs=[any_spec, any_spec, vmem, vmem],
        out_specs=(any_spec, vmem, vmem),
        scratch_shapes=[
            pltpu.VMEM((blocks, rows, pixels), images.dtype),
            pltpu.VMEM((blocks, deep, blocks * rows), jnp.float32),
            pltpu.VMEM((tpl_dev, pixels), templates.dtype),
            pltpu.VMEM((share * pixes, blocks * rows), jnp.float32),
            pltpu.VMEM((pixes - 1, share, blocks * rows), jnp.float32),
            pltpu.VMEM((SWEEPS, 1, blocks * rows), jnp.float32),
            pltpu.VMEM((SWEEPS, devices, 1, blocks * rows), jnp.float32),
            dma((3, blocks)), dma((blocks, CHUNKS)), dma((3, blocks)), dma((blocks,)), dma((4,)),
            dma((pixes - 1,)), dma((pixes - 1,)), dma((SWEEPS,)), dma((SWEEPS,)),
            dma((pixes - 1,)), dma((pixes - 1,)),
        ],
        compiler_params=pltpu.CompilerParams(collective_id=0, has_side_effects=True),
    )(images, templates, info, tlog)
    means = jnp.einsum("ti,ip->tp", plan[:tpl_dev], gath.reshape(blocks * rows, pixels),
                       preferred_element_type=jnp.float32).astype(jnp.bfloat16)
    return means, lax.dynamic_slice(duals.reshape(-1), (b * rows,), (rows,))


def on_device(images, templates, routes, image_weight, template_weight):
    blocks = lax.axis_size("blk")
    if blocks * images.shape[0] <= templates.shape[0] and blocks % LINES == 0:
        return gathered(images, templates, routes, image_weight, template_weight)
    return routed(images, templates, routes, image_weight, template_weight)


def solution(mesh):
    in_specs = (P("blk", "pix"), P("blk", "pix"), P("blk", None), P("blk"), P("blk"))
    out_specs = (P("blk", "pix"), P("blk"))
    return jax.shard_map(
        on_device, mesh=mesh, in_specs=in_specs, out_specs=out_specs, check_vma=False
    )
```

```python
import functools
import jax
import jax.numpy as jnp
from jax import lax
from jax.experimental import pallas as pl
from jax.experimental.pallas import tpu as pltpu
from jax.sharding import PartitionSpec as P

SWEEPS = 2
LINES = 2
CHUNKS = 8
LAG = 2
NEG = -1e30
MESH = pl.DeviceIdType.MESH
UP, DOWN, ACROSS = 0, 1, 2


def routed(images, templates, routes, image_weight, template_weight):
    blocks = lax.axis_size("blk")
    img_dev = images.shape[0]
    admits = routes.shape[1]
    capacity = max(2, (3 * img_dev * admits + 2 * blocks - 1) // (2 * blocks))
    target = routes.reshape(-1)
    target_hot = (target[:, None] == jnp.arange(blocks, dtype=jnp.int32)[None, :]).astype(jnp.int32)
    before = jnp.cumsum(target_hot, axis=0) - target_hot
    position = jnp.sum(before * target_hot, axis=1)
    slot_of = target * capacity + position
    wanted = jnp.arange(blocks * capacity, dtype=jnp.int32)
    matches = slot_of[None, :] == wanted[:, None]
    filled = jnp.any(matches, axis=1)
    owner_image = jnp.sum(
        jnp.where(matches, jnp.arange(target.shape[0], dtype=jnp.int32)[None, :] // admits, 0),
        axis=1,
    )
    outgoing = jnp.where(filled[:, None], images[owner_image], jnp.zeros((), images.dtype))
    outgoing = outgoing.reshape(blocks, capacity, images.shape[1])
    slot_flags = filled.astype(jnp.bfloat16).reshape(blocks, capacity)
    template_log = jnp.log(template_weight)
    arrived_piece = lax.all_to_all(outgoing, "blk", split_axis=0, concat_axis=0, tiled=True)
    marks_piece = lax.all_to_all(slot_flags, "blk", split_axis=0, concat_axis=0, tiled=True)
    partial_value = jnp.einsum(
        "bmp,tp->bmt", arrived_piece, templates, preferred_element_type=jnp.float32
    )
    summed = lax.psum(partial_value, "pix")
    usable = marks_piece > 0
    image_log = jnp.log(image_weight)
    slot_duals = jnp.zeros((blocks, capacity), jnp.float32)
    image_duals = jnp.zeros((img_dev,), jnp.float32)
    for sweep_index in range(SWEEPS):
        column_terms = jnp.where(usable[:, :, None], summed + slot_duals[:, :, None], -jnp.inf)
        column_peak = jnp.max(column_terms, axis=(0, 1))
        template_duals = (
            template_log
            - column_peak
            - jnp.log(jnp.sum(jnp.exp(column_terms - column_peak), axis=(0, 1)))
        )
        row_terms = summed + template_duals
        row_peak = jnp.max(row_terms, axis=2)
        row_total = jnp.sum(jnp.exp(row_terms - row_peak[:, :, None]), axis=2)
        levels = row_peak + jnp.log(row_total)
        back_levels = lax.all_to_all(levels, "blk", split_axis=0, concat_axis=0, tiled=True)
        level_routes = back_levels.reshape(-1)[slot_of].reshape(img_dev, admits)
        route_peak = jnp.max(level_routes, axis=1)
        image_duals = (
            image_log
            - route_peak
            - jnp.log(jnp.sum(jnp.exp(level_routes - route_peak[:, None]), axis=1))
        )
        duals_send = jnp.where(filled, image_duals[owner_image], 0.0).reshape(blocks, capacity)
        slot_duals = lax.all_to_all(duals_send, "blk", split_axis=0, concat_axis=0, tiled=True)
    column_terms = jnp.where(usable[:, :, None], summed + slot_duals[:, :, None], -jnp.inf)
    column_peak = jnp.max(column_terms, axis=(0, 1))
    column_exp = jnp.exp(column_terms - column_peak)
    plan_weights = (column_exp / jnp.sum(column_exp, axis=(0, 1))).astype(jnp.bfloat16)
    template_means = jnp.einsum(
        "bmt,bmp->tp", plan_weights, arrived_piece, preferred_element_type=jnp.float32
    ).astype(jnp.bfloat16)
    return (template_means, image_duals)


def gather_and_plan(dims, img_hbm, tpl_hbm, routes_ref, iw_ref, tw_ref, gath_hbm, plan_ref, dual_ref,
                    buf, infos, tpl, acc, parts, lse_out, lse_in,
                    send_sem, recv_sem, info_send, info_recv, local_sem,
                    part_send, part_recv, lse_send, lse_recv, plan_send, plan_recv):
    blocks, pixes, admits, tpl_dev, share = dims
    depth = blocks // LINES
    rows, pixels = img_hbm.shape
    width = pixels // CHUNKS
    b, p = lax.axis_index("blk"), lax.axis_index("pix")
    z, y = b // LINES, b % LINES
    other = 1 - y
    has_up, has_down = z < depth - 1, z > 0
    target = {UP: b + LINES, DOWN: b - LINES, ACROSS: z * LINES + other}
    allowed = {UP: has_up, DOWN: has_down}

    tpl_copy = pltpu.make_async_copy(tpl_hbm, tpl, local_sem.at[0])
    tpl_copy.start()

    names = routes_ref[...].astype(jnp.float32) + 1.0
    logs = jnp.log(iw_ref[...])
    infos[b] = jnp.zeros(infos.shape[1:], jnp.float32)
    for k in range(blocks):
        window = slice(k * rows, (k + 1) * rows)
        infos[b, 0:admits, window] = jnp.where(b == k, names, 0.0)
        infos[b, admits:admits + 1, window] = jnp.where(b == k, logs, 0.0)

    barrier = pltpu.get_barrier_semaphore()
    for way in (UP, DOWN):
        @pl.when(allowed[way])
        def _():
            pl.semaphore_signal(barrier, inc=1, device_id={"blk": target[way]}, device_id_type=MESH)
    pl.semaphore_signal(barrier, inc=1, device_id={"blk": target[ACROSS]}, device_id_type=MESH)
    for j in range(1, pixes):
        pl.semaphore_signal(barrier, inc=1, device_id={"pix": lax.rem(p + j, pixes)}, device_id_type=MESH)
    near = jnp.where(has_up, 1, 0) + jnp.where(has_down, 1, 0) + pixes
    pl.semaphore_wait(barrier, near)

    def cols(c):
        return pl.ds(c * width, width)

    def piece(way, k, c, own=False):
        return pltpu.make_async_remote_copy(
            src_ref=img_hbm.at[:, cols(c)] if own else buf.at[c, k],
            dst_ref=buf.at[c, k],
            send_sem=send_sem.at[way, k], recv_sem=recv_sem.at[k, c],
            device_id={"blk": target[way]}, device_id_type=MESH)

    def info_piece(way, k):
        return pltpu.make_async_remote_copy(
            src_ref=infos.at[k], dst_ref=infos.at[k],
            send_sem=info_send.at[way, k], recv_sem=info_recv.at[k],
            device_id={"blk": target[way]}, device_id_type=MESH)

    def arrived(k, c):
        pltpu.make_async_copy(buf.at[c, k], buf.at[c, k], recv_sem.at[k, c]).wait()

    def info_arrived(k):
        pltpu.make_async_copy(infos.at[k], infos.at[k], info_recv.at[k]).wait()

    def along(way, start):
        @pl.when(allowed[way])
        def _():
            start()

    for c in range(CHUNKS):
        piece(ACROSS, b, c, True).start()
        for way in (UP, DOWN):
            along(way, lambda: piece(way, b, c, True).start())
    for c in range(CHUNKS):
        pltpu.make_async_copy(img_hbm.at[:, cols(c)], buf.at[c, b], local_sem.at[1]).start()
    info_piece(ACROSS, b).start()
    for way in (UP, DOWN):
        along(way, lambda: info_piece(way, b).start())
    mate = z * LINES + other
    arrived(mate, 0)
    for way in (UP, DOWN):
        along(way, lambda: piece(way, mate, 0).start())

    def sides(d):
        return ((UP, z - d, z >= d), (DOWN, z + d, z + d < depth))

    def pass_on(d, c):
        for way, from_z, there in sides(d):
            k = from_z * LINES + y

            @pl.when(there)
            def _():
                arrived(k, c)
                if c:
                    piece(ACROSS, k, c).start()
                along(way, lambda: piece(way, k, c).start())

    def pass_rest(d):
        for way, from_z, there in sides(d):
            k, k2 = from_z * LINES + y, from_z * LINES + other

            @pl.when(there)
            def _():
                arrived(k2, 0)
                along(way, lambda: piece(way, k2, 0).start())
                info_arrived(k)
                info_piece(ACROSS, k).start()
                along(way, lambda: info_piece(way, k).start())

    def crossed(c):
        if c:
            arrived(mate, c)
            for d in range(1, depth):
                for way, from_z, there in sides(d):
                    @pl.when(there)
                    def _():
                        arrived(from_z * LINES + other, c)

    def product(c):
        images = buf[c].reshape(blocks * rows, width)
        term = lax.dot_general(tpl[:, c * width:(c + 1) * width], images, (((1,), (1,)), ((), ())),
                               preferred_element_type=jnp.float32)
        if c == 1:
            acc[0:tpl_dev, :] = term
        else:
            acc[0:tpl_dev, :] += term

    for d in range(1, depth - 1):
        for c in range(CHUNKS):
            pass_on(d, c)
        pass_rest(d)
    pltpu.make_async_copy(buf.at[:, b], buf.at[:, b], local_sem.at[1]).wait()
    tpl_copy.wait()
    if share * pixes > tpl_dev:
        acc[tpl_dev:, :] = jnp.zeros((share * pixes - tpl_dev, blocks * rows), jnp.float32)
    for c in range(CHUNKS + LAG):
        if c < CHUNKS:
            pass_on(depth - 1, c)
        if c == CHUNKS - 1:
            pass_rest(depth - 1)
        if c == CHUNKS + LAG - 1:
            product(0)
        if c > LAG:
            crossed(c - LAG)
            product(c - LAG)

    def my_part(j):
        return pltpu.make_async_remote_copy(
            src_ref=acc.at[pl.ds(lax.rem(p + j, pixes) * share, share), :], dst_ref=parts.at[j - 1],
            send_sem=part_send.at[j - 1], recv_sem=part_recv.at[j - 1],
            device_id={"pix": lax.rem(p + j, pixes)}, device_id_type=MESH)

    for j in range(1, pixes):
        my_part(j).start()
    back = pltpu.make_async_copy(buf, gath_hbm, local_sem.at[3])
    back.start()

    info_arrived(mate)
    for d in range(1, depth):
        for way, from_z, there in sides(d):
            @pl.when(there)
            def _():
                info_arrived(from_z * LINES + other)
    info = jnp.sum(infos[...], axis=0)
    code = (b + 1).astype(jnp.float32)
    admitted = jnp.max(jnp.where(info[0:admits, :] == code, 1.0, 0.0), axis=0, keepdims=True)
    image_log = info[admits:admits + 1, :]
    first = p * share
    here = (lax.broadcasted_iota(jnp.int32, (share, tpl_dev), 0) + first
            == lax.broadcasted_iota(jnp.int32, (share, tpl_dev), 1))
    template_log = jnp.sum(jnp.where(here, jnp.log(tw_ref[...]), 0.0), axis=1, keepdims=True)
    valid = first + lax.broadcasted_iota(jnp.int32, (share, 1), 0) < tpl_dev
    scores = acc[pl.ds(pl.multiple_of(first, 16), share), :]
    for j in range(1, pixes):
        my_part(j).wait_recv()
        scores = scores + parts[j - 1]
    scores = jnp.where(admitted > 0, scores, NEG)

    me = b * pixes + p
    devices = blocks * pixes
    duals = jnp.zeros((1, blocks * rows), jnp.float32)
    for sweep in range(SWEEPS):
        terms = scores + duals
        peak = jnp.max(terms, axis=1, keepdims=True)
        level = template_log - peak - jnp.log(jnp.sum(jnp.exp(terms - peak), axis=1, keepdims=True))
        level = jnp.where(valid, level, NEG)
        terms = scores + level
        peak = jnp.max(terms, axis=0, keepdims=True)
        lse = peak + jnp.log(jnp.sum(jnp.exp(terms - peak), axis=0, keepdims=True))
        lse_out[sweep] = lse

        def post(j, carry):
            to = lax.rem(me + j, devices)
            pltpu.make_async_remote_copy(
                src_ref=lse_out.at[sweep], dst_ref=lse_in.at[sweep, me],
                send_sem=lse_send.at[sweep], recv_sem=lse_recv.at[sweep],
                device_id={"blk": to // pixes, "pix": lax.rem(to, pixes)}, device_id_type=MESH).start()
            return carry

        lax.fori_loop(1, devices, post, 0)
        lse_in[sweep, me] = lse
        span = lse_in.at[sweep, pl.ds(0, devices - 1)]
        pltpu.make_async_copy(span, span, lse_recv.at[sweep]).wait()
        every = lse_in[sweep]
        peak = jnp.max(every, axis=0)
        duals = image_log - peak - jnp.log(jnp.sum(jnp.exp(every - peak), axis=0))
    mine_only = jnp.zeros((1, rows), jnp.float32)
    for k in range(blocks):
        mine_only = jnp.where(b == k, duals[:, k * rows:(k + 1) * rows], mine_only)
    dual_ref[...] = mine_only
    terms = scores + duals
    weight = jnp.exp(terms - jnp.max(terms, axis=1, keepdims=True))
    mine = pl.ds(pl.multiple_of(first, 16), share)
    plan_ref[mine, :] = (weight / jnp.sum(weight, axis=1, keepdims=True)).astype(jnp.bfloat16)

    def my_plan(j):
        return pltpu.make_async_remote_copy(
            src_ref=plan_ref.at[mine, :], dst_ref=plan_ref.at[mine, :],
            send_sem=plan_send.at[j - 1], recv_sem=plan_recv.at[j - 1],
            device_id={"pix": lax.rem(p + j, pixes)}, device_id_type=MESH)

    for j in range(1, pixes):
        my_plan(j).start()

    full = buf.at[:, b]
    rest = buf.at[pl.ds(1, CHUNKS - 1), b]
    one = buf.at[0, b]

    def left(ref, sem):
        pltpu.make_async_copy(ref, ref, sem).wait()

    left(full, send_sem.at[ACROSS, b])
    left(infos.at[b], info_send.at[ACROSS, b])
    for way in (UP, DOWN):
        along(way, lambda: (left(full, send_sem.at[way, b]), left(one, send_sem.at[way, mate]),
                            left(infos.at[b], info_send.at[way, b])) and None)
    for d in range(1, depth):
        for way, from_z, there in sides(d):
            k, k2 = from_z * LINES + y, from_z * LINES + other

            @pl.when(there)
            def _():
                left(rest, send_sem.at[ACROSS, k])
                left(infos.at[b], info_send.at[ACROSS, k])
                along(way, lambda: (left(full, send_sem.at[way, k]), left(one, send_sem.at[way, k2]),
                                    left(infos.at[b], info_send.at[way, k])) and None)
    for j in range(1, pixes):
        my_part(j).wait_send()
    for sweep in range(SWEEPS):
        span = lse_in.at[sweep, pl.ds(0, devices - 1)]
        left(span, lse_send.at[sweep])
    back.wait()
    for j in range(1, pixes):
        my_plan(j).wait_send()
        my_plan(j).wait_recv()


def average(plan_ref, img_ref, out_ref):
    _, blocks, rows, width = img_ref.shape
    images = img_ref[0].reshape(blocks * rows, width)
    out_ref[...] = jnp.dot(plan_ref[0:out_ref.shape[0], :], images,
                           preferred_element_type=jnp.float32).astype(out_ref.dtype)


def gathered(images, templates, routes, image_weight, template_weight):
    blocks, pixes = lax.axis_size("blk"), lax.axis_size("pix")
    rows, pixels = images.shape
    tpl_dev, admits = templates.shape[0], routes.shape[1]
    share = -(-tpl_dev // (16 * pixes)) * 16
    deep = -(-(admits + 1) // 8) * 8
    width = pixels // CHUNKS
    dims = (blocks, pixes, admits, tpl_dev, share)
    any_spec, vmem = pl.BlockSpec(memory_space=pl.ANY), pl.BlockSpec(memory_space=pltpu.VMEM)
    dma = pltpu.SemaphoreType.DMA
    devices = blocks * pixes
    gath, plan, duals = pl.pallas_call(
        functools.partial(gather_and_plan, dims),
        out_shape=(jax.ShapeDtypeStruct((CHUNKS, blocks, rows, width), images.dtype),
                   jax.ShapeDtypeStruct((share * pixes, blocks * rows), jnp.bfloat16),
                   jax.ShapeDtypeStruct((1, rows), jnp.float32)),
        in_specs=[any_spec, any_spec, vmem, vmem, vmem],
        out_specs=(any_spec, vmem, vmem),
        scratch_shapes=[
            pltpu.VMEM((CHUNKS, blocks, rows, width), images.dtype),
            pltpu.VMEM((blocks, deep, blocks * rows), jnp.float32),
            pltpu.VMEM((tpl_dev, pixels), templates.dtype),
            pltpu.VMEM((share * pixes, blocks * rows), jnp.float32),
            pltpu.VMEM((pixes - 1, share, blocks * rows), jnp.float32),
            pltpu.VMEM((SWEEPS, 1, blocks * rows), jnp.float32),
            pltpu.VMEM((SWEEPS, devices, 1, blocks * rows), jnp.float32),
            dma((3, blocks)), dma((blocks, CHUNKS)), dma((3, blocks)), dma((blocks,)), dma((4,)),
            dma((pixes - 1,)), dma((pixes - 1,)), dma((SWEEPS,)), dma((SWEEPS,)),
            dma((pixes - 1,)), dma((pixes - 1,)),
        ],
        compiler_params=pltpu.CompilerParams(collective_id=0, has_side_effects=True),
    )(images, templates, routes.T, image_weight[None, :], template_weight[None, :])
    means = pl.pallas_call(
        average,
        grid=(CHUNKS,),
        out_shape=jax.ShapeDtypeStruct((tpl_dev, pixels), jnp.bfloat16),
        in_specs=[pl.BlockSpec((share * pixes, blocks * rows), lambda c: (0, 0)),
                  pl.BlockSpec((1, blocks, rows, width), lambda c: (c, 0, 0, 0))],
        out_specs=pl.BlockSpec((tpl_dev, width), lambda c: (0, c)),
    )(plan, gath)
    return means, duals.reshape(-1)


def on_device(images, templates, routes, image_weight, template_weight):
    blocks = lax.axis_size("blk")
    if blocks * images.shape[0] <= templates.shape[0] and blocks % LINES == 0:
        return gathered(images, templates, routes, image_weight, template_weight)
    return routed(images, templates, routes, image_weight, template_weight)


def solution(mesh):
    in_specs = (P("blk", "pix"), P("blk", "pix"), P("blk", None), P("blk"), P("blk"))
    out_specs = (P("blk", "pix"), P("blk"))
    return jax.shard_map(
        on_device, mesh=mesh, in_specs=in_specs, out_specs=out_specs, check_vma=False
    )
```

```python
import functools
import jax
import jax.numpy as jnp
from jax import lax
from jax.experimental import pallas as pl
from jax.experimental.pallas import tpu as pltpu
from jax.sharding import PartitionSpec as P

SWEEPS = 2
LINES = 2
CHUNKS = 8
LAG = 2
NEG = -1e30
MESH = pl.DeviceIdType.MESH
UP, DOWN, ACROSS = 0, 1, 2


def routed(images, templates, routes, image_weight, template_weight):
    blocks = lax.axis_size("blk")
    img_dev = images.shape[0]
    admits = routes.shape[1]
    capacity = max(2, (3 * img_dev * admits + 2 * blocks - 1) // (2 * blocks))
    target = routes.reshape(-1)
    target_hot = (target[:, None] == jnp.arange(blocks, dtype=jnp.int32)[None, :]).astype(jnp.int32)
    before = jnp.cumsum(target_hot, axis=0) - target_hot
    position = jnp.sum(before * target_hot, axis=1)
    slot_of = target * capacity + position
    wanted = jnp.arange(blocks * capacity, dtype=jnp.int32)
    matches = slot_of[None, :] == wanted[:, None]
    filled = jnp.any(matches, axis=1)
    owner_image = jnp.sum(
        jnp.where(matches, jnp.arange(target.shape[0], dtype=jnp.int32)[None, :] // admits, 0),
        axis=1,
    )
    outgoing = jnp.where(filled[:, None], images[owner_image], jnp.zeros((), images.dtype))
    outgoing = outgoing.reshape(blocks, capacity, images.shape[1])
    slot_flags = filled.astype(jnp.bfloat16).reshape(blocks, capacity)
    template_log = jnp.log(template_weight)
    arrived_piece = lax.all_to_all(outgoing, "blk", split_axis=0, concat_axis=0, tiled=True)
    marks_piece = lax.all_to_all(slot_flags, "blk", split_axis=0, concat_axis=0, tiled=True)
    partial_value = jnp.einsum(
        "bmp,tp->bmt", arrived_piece, templates, preferred_element_type=jnp.float32
    )
    summed = lax.psum(partial_value, "pix")
    usable = marks_piece > 0
    image_log = jnp.log(image_weight)
    slot_duals = jnp.zeros((blocks, capacity), jnp.float32)
    image_duals = jnp.zeros((img_dev,), jnp.float32)
    for sweep_index in range(SWEEPS):
        column_terms = jnp.where(usable[:, :, None], summed + slot_duals[:, :, None], -jnp.inf)
        column_peak = jnp.max(column_terms, axis=(0, 1))
        template_duals = (
            template_log
            - column_peak
            - jnp.log(jnp.sum(jnp.exp(column_terms - column_peak), axis=(0, 1)))
        )
        row_terms = summed + template_duals
        row_peak = jnp.max(row_terms, axis=2)
        row_total = jnp.sum(jnp.exp(row_terms - row_peak[:, :, None]), axis=2)
        levels = row_peak + jnp.log(row_total)
        back_levels = lax.all_to_all(levels, "blk", split_axis=0, concat_axis=0, tiled=True)
        level_routes = back_levels.reshape(-1)[slot_of].reshape(img_dev, admits)
        route_peak = jnp.max(level_routes, axis=1)
        image_duals = (
            image_log
            - route_peak
            - jnp.log(jnp.sum(jnp.exp(level_routes - route_peak[:, None]), axis=1))
        )
        duals_send = jnp.where(filled, image_duals[owner_image], 0.0).reshape(blocks, capacity)
        slot_duals = lax.all_to_all(duals_send, "blk", split_axis=0, concat_axis=0, tiled=True)
    column_terms = jnp.where(usable[:, :, None], summed + slot_duals[:, :, None], -jnp.inf)
    column_peak = jnp.max(column_terms, axis=(0, 1))
    column_exp = jnp.exp(column_terms - column_peak)
    plan_weights = (column_exp / jnp.sum(column_exp, axis=(0, 1))).astype(jnp.bfloat16)
    template_means = jnp.einsum(
        "bmt,bmp->tp", plan_weights, arrived_piece, preferred_element_type=jnp.float32
    ).astype(jnp.bfloat16)
    return (template_means, image_duals)


def gather_and_plan(dims, img_hbm, tpl_hbm, routes_ref, iw_ref, tw_ref, gath_hbm, plan_ref, dual_ref,
                    buf, infos, tpl, acc, parts, lse_out, lse_in,
                    send_sem, recv_sem, info_send, info_recv, local_sem,
                    part_send, part_recv, lse_send, lse_recv, plan_send, plan_recv):
    blocks, pixes, admits, tpl_dev, share = dims
    depth = blocks // LINES
    rows, pixels = img_hbm.shape
    width = pixels // CHUNKS
    b, p = lax.axis_index("blk"), lax.axis_index("pix")
    z, y = b // LINES, b % LINES
    other = 1 - y
    has_up, has_down = z < depth - 1, z > 0
    target = {UP: b + LINES, DOWN: b - LINES, ACROSS: z * LINES + other}
    allowed = {UP: has_up, DOWN: has_down}

    tpl_copy = pltpu.make_async_copy(tpl_hbm, tpl, local_sem.at[0])
    tpl_copy.start()

    names = routes_ref[...].astype(jnp.float32) + 1.0
    logs = jnp.log(iw_ref[...])
    infos[b] = jnp.zeros(infos.shape[1:], jnp.float32)
    for k in range(blocks):
        window = slice(k * rows, (k + 1) * rows)
        infos[b, 0:admits, window] = jnp.where(b == k, names, 0.0)
        infos[b, admits:admits + 1, window] = jnp.where(b == k, logs, 0.0)

    barrier = pltpu.get_barrier_semaphore()
    for way in (UP, DOWN):
        @pl.when(allowed[way])
        def _():
            pl.semaphore_signal(barrier, inc=1, device_id={"blk": target[way]}, device_id_type=MESH)
    pl.semaphore_signal(barrier, inc=1, device_id={"blk": target[ACROSS]}, device_id_type=MESH)
    for j in range(1, pixes):
        pl.semaphore_signal(barrier, inc=1, device_id={"pix": lax.rem(p + j, pixes)}, device_id_type=MESH)
    near = jnp.where(has_up, 1, 0) + jnp.where(has_down, 1, 0) + pixes
    pl.semaphore_wait(barrier, near)

    def cols(c):
        return pl.ds(c * width, width)

    def piece(way, k, c, own=False):
        return pltpu.make_async_remote_copy(
            src_ref=img_hbm.at[:, cols(c)] if own else buf.at[c, k],
            dst_ref=buf.at[c, k],
            send_sem=send_sem.at[way, k], recv_sem=recv_sem.at[k, c],
            device_id={"blk": target[way]}, device_id_type=MESH)

    def info_piece(way, k):
        return pltpu.make_async_remote_copy(
            src_ref=infos.at[k], dst_ref=infos.at[k],
            send_sem=info_send.at[way, k], recv_sem=info_recv.at[k],
            device_id={"blk": target[way]}, device_id_type=MESH)

    def arrived(k, c):
        pltpu.make_async_copy(buf.at[c, k], buf.at[c, k], recv_sem.at[k, c]).wait()

    def info_arrived(k):
        pltpu.make_async_copy(infos.at[k], infos.at[k], info_recv.at[k]).wait()

    def along(way, start):
        @pl.when(allowed[way])
        def _():
            start()

    for c in range(CHUNKS):
        piece(ACROSS, b, c, True).start()
        for way in (UP, DOWN):
            along(way, lambda: piece(way, b, c, True).start())
    for c in range(CHUNKS):
        pltpu.make_async_copy(img_hbm.at[:, cols(c)], buf.at[c, b], local_sem.at[1]).start()
    info_piece(ACROSS, b).start()
    for way in (UP, DOWN):
        along(way, lambda: info_piece(way, b).start())
    mate = z * LINES + other
    arrived(mate, 0)
    for way in (UP, DOWN):
        along(way, lambda: piece(way, mate, 0).start())

    def sides(d):
        return ((UP, z - d, z >= d), (DOWN, z + d, z + d < depth))

    def pass_on(d, c):
        for way, from_z, there in sides(d):
            k = from_z * LINES + y

            @pl.when(there)
            def _():
                arrived(k, c)
                if c:
                    piece(ACROSS, k, c).start()
                along(way, lambda: piece(way, k, c).start())

    def pass_rest(d):
        for way, from_z, there in sides(d):
            k, k2 = from_z * LINES + y, from_z * LINES + other

            @pl.when(there)
            def _():
                arrived(k2, 0)
                along(way, lambda: piece(way, k2, 0).start())
                info_arrived(k)
                info_piece(ACROSS, k).start()
                along(way, lambda: info_piece(way, k).start())

    def crossed(c):
        if c:
            arrived(mate, c)
            for d in range(1, depth):
                for way, from_z, there in sides(d):
                    @pl.when(there)
                    def _():
                        arrived(from_z * LINES + other, c)

    def product(c):
        images = buf[c].reshape(blocks * rows, width)
        term = lax.dot_general(tpl[:, c * width:(c + 1) * width], images, (((1,), (1,)), ((), ())),
                               preferred_element_type=jnp.float32)
        if c == 1:
            acc[0:tpl_dev, :] = term
        else:
            acc[0:tpl_dev, :] += term

    for d in range(1, depth - 1):
        for c in range(CHUNKS):
            pass_on(d, c)
        pass_rest(d)
    pltpu.make_async_copy(buf.at[:, b], buf.at[:, b], local_sem.at[1]).wait()
    tpl_copy.wait()
    if share * pixes > tpl_dev:
        acc[tpl_dev:, :] = jnp.zeros((share * pixes - tpl_dev, blocks * rows), jnp.float32)
    for c in range(CHUNKS + LAG):
        if c < CHUNKS:
            pass_on(depth - 1, c)
        if c == CHUNKS - 1:
            pass_rest(depth - 1)
        if c == CHUNKS + LAG - 1:
            product(0)
        if c > LAG:
            crossed(c - LAG)
            product(c - LAG)

    def my_part(j):
        return pltpu.make_async_remote_copy(
            src_ref=acc.at[pl.ds(lax.rem(p + j, pixes) * share, share), :], dst_ref=parts.at[j - 1],
            send_sem=part_send.at[j - 1], recv_sem=part_recv.at[j - 1],
            device_id={"pix": lax.rem(p + j, pixes)}, device_id_type=MESH)

    for j in range(1, pixes):
        my_part(j).start()
    for c in range(CHUNKS):
        pltpu.make_async_copy(buf.at[c], gath_hbm.at[:, :, cols(c)], local_sem.at[3]).start()

    info_arrived(mate)
    for d in range(1, depth):
        for way, from_z, there in sides(d):
            @pl.when(there)
            def _():
                info_arrived(from_z * LINES + other)
    info = jnp.sum(infos[...], axis=0)
    code = (b + 1).astype(jnp.float32)
    admitted = jnp.max(jnp.where(info[0:admits, :] == code, 1.0, 0.0), axis=0, keepdims=True)
    image_log = info[admits:admits + 1, :]
    first = p * share
    here = (lax.broadcasted_iota(jnp.int32, (share, tpl_dev), 0) + first
            == lax.broadcasted_iota(jnp.int32, (share, tpl_dev), 1))
    template_log = jnp.sum(jnp.where(here, jnp.log(tw_ref[...].reshape(1, tpl_dev)), 0.0), axis=1, keepdims=True)
    valid = first + lax.broadcasted_iota(jnp.int32, (share, 1), 0) < tpl_dev
    scores = acc[pl.ds(pl.multiple_of(first, 16), share), :]
    for j in range(1, pixes):
        my_part(j).wait_recv()
        scores = scores + parts[j - 1]
    scores = jnp.where(admitted > 0, scores, NEG)

    me = b * pixes + p
    devices = blocks * pixes
    duals = jnp.zeros((1, blocks * rows), jnp.float32)
    for sweep in range(SWEEPS):
        terms = scores + duals
        peak = jnp.max(terms, axis=1, keepdims=True)
        level = template_log - peak - jnp.log(jnp.sum(jnp.exp(terms - peak), axis=1, keepdims=True))
        level = jnp.where(valid, level, NEG)
        terms = scores + level
        peak = jnp.max(terms, axis=0, keepdims=True)
        lse = peak + jnp.log(jnp.sum(jnp.exp(terms - peak), axis=0, keepdims=True))
        lse_out[sweep] = lse

        def post(j, carry):
            to = lax.rem(me + j, devices)
            pltpu.make_async_remote_copy(
                src_ref=lse_out.at[sweep], dst_ref=lse_in.at[sweep, me],
                send_sem=lse_send.at[sweep], recv_sem=lse_recv.at[sweep],
                device_id={"blk": to // pixes, "pix": lax.rem(to, pixes)}, device_id_type=MESH).start()
            return carry

        lax.fori_loop(1, devices, post, 0)
        lse_in[sweep, me] = lse
        span = lse_in.at[sweep, pl.ds(0, devices - 1)]
        pltpu.make_async_copy(span, span, lse_recv.at[sweep]).wait()
        every = lse_in[sweep]
        peak = jnp.max(every, axis=0)
        duals = image_log - peak - jnp.log(jnp.sum(jnp.exp(every - peak), axis=0))
    mine_only = jnp.zeros((1, rows), jnp.float32)
    for k in range(blocks):
        mine_only = jnp.where(b == k, duals[:, k * rows:(k + 1) * rows], mine_only)
    dual_ref[...] = mine_only
    terms = scores + duals
    weight = jnp.exp(terms - jnp.max(terms, axis=1, keepdims=True))
    mine = pl.ds(pl.multiple_of(first, 16), share)
    plan_ref[mine, :] = (weight / jnp.sum(weight, axis=1, keepdims=True)).astype(jnp.bfloat16)

    def my_plan(j):
        return pltpu.make_async_remote_copy(
            src_ref=plan_ref.at[mine, :], dst_ref=plan_ref.at[mine, :],
            send_sem=plan_send.at[j - 1], recv_sem=plan_recv.at[j - 1],
            device_id={"pix": lax.rem(p + j, pixes)}, device_id_type=MESH)

    for j in range(1, pixes):
        my_plan(j).start()

    full = buf.at[:, b]
    rest = buf.at[pl.ds(1, CHUNKS - 1), b]
    one = buf.at[0, b]

    def left(ref, sem):
        pltpu.make_async_copy(ref, ref, sem).wait()

    left(full, send_sem.at[ACROSS, b])
    left(infos.at[b], info_send.at[ACROSS, b])
    for way in (UP, DOWN):
        along(way, lambda: (left(full, send_sem.at[way, b]), left(one, send_sem.at[way, mate]),
                            left(infos.at[b], info_send.at[way, b])) and None)
    for d in range(1, depth):
        for way, from_z, there in sides(d):
            k, k2 = from_z * LINES + y, from_z * LINES + other

            @pl.when(there)
            def _():
                left(rest, send_sem.at[ACROSS, k])
                left(infos.at[b], info_send.at[ACROSS, k])
                along(way, lambda: (left(full, send_sem.at[way, k]), left(one, send_sem.at[way, k2]),
                                    left(infos.at[b], info_send.at[way, k])) and None)
    for j in range(1, pixes):
        my_part(j).wait_send()
    for sweep in range(SWEEPS):
        span = lse_in.at[sweep, pl.ds(0, devices - 1)]
        left(span, lse_send.at[sweep])
    left(buf, local_sem.at[3])
    for j in range(1, pixes):
        my_plan(j).wait_send()
        my_plan(j).wait_recv()


def gathered(images, templates, routes, image_weight, template_weight):
    blocks, pixes = lax.axis_size("blk"), lax.axis_size("pix")
    rows, pixels = images.shape
    tpl_dev, admits = templates.shape[0], routes.shape[1]
    share = -(-tpl_dev // (16 * pixes)) * 16
    deep = -(-(admits + 1) // 8) * 8
    width = pixels // CHUNKS
    dims = (blocks, pixes, admits, tpl_dev, share)
    any_spec, vmem = pl.BlockSpec(memory_space=pl.ANY), pl.BlockSpec(memory_space=pltpu.VMEM)
    dma = pltpu.SemaphoreType.DMA
    devices = blocks * pixes
    gath, plan, duals = pl.pallas_call(
        functools.partial(gather_and_plan, dims),
        out_shape=(jax.ShapeDtypeStruct((blocks, rows, pixels), images.dtype),
                   jax.ShapeDtypeStruct((share * pixes, blocks * rows), jnp.bfloat16),
                   jax.ShapeDtypeStruct((1, rows), jnp.float32)),
        in_specs=[any_spec, any_spec, vmem, vmem, vmem],
        out_specs=(any_spec, vmem, vmem),
        scratch_shapes=[
            pltpu.VMEM((CHUNKS, blocks, rows, width), images.dtype),
            pltpu.VMEM((blocks, deep, blocks * rows), jnp.float32),
            pltpu.VMEM((tpl_dev, pixels), templates.dtype),
            pltpu.VMEM((share * pixes, blocks * rows), jnp.float32),
            pltpu.VMEM((pixes - 1, share, blocks * rows), jnp.float32),
            pltpu.VMEM((SWEEPS, 1, blocks * rows), jnp.float32),
            pltpu.VMEM((SWEEPS, devices, 1, blocks * rows), jnp.float32),
            dma((3, blocks)), dma((blocks, CHUNKS)), dma((3, blocks)), dma((blocks,)), dma((4,)),
            dma((pixes - 1,)), dma((pixes - 1,)), dma((SWEEPS,)), dma((SWEEPS,)),
            dma((pixes - 1,)), dma((pixes - 1,)),
        ],
        compiler_params=pltpu.CompilerParams(collective_id=0, has_side_effects=True),
    )(images, templates, routes.T, image_weight[None, :], template_weight)
    means = jnp.einsum("ti,ip->tp", plan[:tpl_dev], gath.reshape(blocks * rows, pixels),
                       preferred_element_type=jnp.float32).astype(jnp.bfloat16)
    return means, duals.reshape(-1)


def on_device(images, templates, routes, image_weight, template_weight):
    blocks = lax.axis_size("blk")
    if blocks * images.shape[0] <= templates.shape[0] and blocks % LINES == 0:
        return gathered(images, templates, routes, image_weight, template_weight)
    return routed(images, templates, routes, image_weight, template_weight)


def solution(mesh):
    in_specs = (P("blk", "pix"), P("blk", "pix"), P("blk", None), P("blk"), P("blk"))
    out_specs = (P("blk", "pix"), P("blk"))
    return jax.shard_map(
        on_device, mesh=mesh, in_specs=in_specs, out_specs=out_specs, check_vma=False
    )
```

```python
import functools
import jax
import jax.numpy as jnp
from jax import lax
from jax.experimental import pallas as pl
from jax.experimental.pallas import tpu as pltpu
from jax.sharding import PartitionSpec as P

SWEEPS = 2
LINES = 2
CHUNKS = 8
LAG = 2
NEG = -1e30
MESH = pl.DeviceIdType.MESH
UP, DOWN, ACROSS = 0, 1, 2


def routed(images, templates, routes, image_weight, template_weight):
    blocks = lax.axis_size("blk")
    img_dev = images.shape[0]
    admits = routes.shape[1]
    capacity = max(2, (3 * img_dev * admits + 2 * blocks - 1) // (2 * blocks))
    target = routes.reshape(-1)
    target_hot = (target[:, None] == jnp.arange(blocks, dtype=jnp.int32)[None, :]).astype(jnp.int32)
    before = jnp.cumsum(target_hot, axis=0) - target_hot
    position = jnp.sum(before * target_hot, axis=1)
    slot_of = target * capacity + position
    wanted = jnp.arange(blocks * capacity, dtype=jnp.int32)
    matches = slot_of[None, :] == wanted[:, None]
    filled = jnp.any(matches, axis=1)
    owner_image = jnp.sum(
        jnp.where(matches, jnp.arange(target.shape[0], dtype=jnp.int32)[None, :] // admits, 0),
        axis=1,
    )
    outgoing = jnp.where(filled[:, None], images[owner_image], jnp.zeros((), images.dtype))
    outgoing = outgoing.reshape(blocks, capacity, images.shape[1])
    slot_flags = filled.astype(jnp.bfloat16).reshape(blocks, capacity)
    template_log = jnp.log(template_weight)
    arrived_piece = lax.all_to_all(outgoing, "blk", split_axis=0, concat_axis=0, tiled=True)
    marks_piece = lax.all_to_all(slot_flags, "blk", split_axis=0, concat_axis=0, tiled=True)
    partial_value = jnp.einsum(
        "bmp,tp->bmt", arrived_piece, templates, preferred_element_type=jnp.float32
    )
    summed = lax.psum(partial_value, "pix")
    usable = marks_piece > 0
    image_log = jnp.log(image_weight)
    slot_duals = jnp.zeros((blocks, capacity), jnp.float32)
    image_duals = jnp.zeros((img_dev,), jnp.float32)
    for sweep_index in range(SWEEPS):
        column_terms = jnp.where(usable[:, :, None], summed + slot_duals[:, :, None], -jnp.inf)
        column_peak = jnp.max(column_terms, axis=(0, 1))
        template_duals = (
            template_log
            - column_peak
            - jnp.log(jnp.sum(jnp.exp(column_terms - column_peak), axis=(0, 1)))
        )
        row_terms = summed + template_duals
        row_peak = jnp.max(row_terms, axis=2)
        row_total = jnp.sum(jnp.exp(row_terms - row_peak[:, :, None]), axis=2)
        levels = row_peak + jnp.log(row_total)
        back_levels = lax.all_to_all(levels, "blk", split_axis=0, concat_axis=0, tiled=True)
        level_routes = back_levels.reshape(-1)[slot_of].reshape(img_dev, admits)
        route_peak = jnp.max(level_routes, axis=1)
        image_duals = (
            image_log
            - route_peak
            - jnp.log(jnp.sum(jnp.exp(level_routes - route_peak[:, None]), axis=1))
        )
        duals_send = jnp.where(filled, image_duals[owner_image], 0.0).reshape(blocks, capacity)
        slot_duals = lax.all_to_all(duals_send, "blk", split_axis=0, concat_axis=0, tiled=True)
    column_terms = jnp.where(usable[:, :, None], summed + slot_duals[:, :, None], -jnp.inf)
    column_peak = jnp.max(column_terms, axis=(0, 1))
    column_exp = jnp.exp(column_terms - column_peak)
    plan_weights = (column_exp / jnp.sum(column_exp, axis=(0, 1))).astype(jnp.bfloat16)
    template_means = jnp.einsum(
        "bmt,bmp->tp", plan_weights, arrived_piece, preferred_element_type=jnp.float32
    ).astype(jnp.bfloat16)
    return (template_means, image_duals)


def gather_and_plan(dims, img_hbm, tpl_hbm, routes_ref, iw_ref, tw_ref, gath_hbm, plan_ref, dual_ref,
                    buf, infos, tpl, acc, parts, lse_out, lse_in,
                    send_sem, recv_sem, info_send, info_recv, local_sem,
                    part_send, part_recv, lse_send, lse_recv, plan_send, plan_recv):
    blocks, pixes, admits, tpl_dev, share = dims
    depth = blocks // LINES
    rows, pixels = img_hbm.shape
    width = pixels // CHUNKS
    b, p = lax.axis_index("blk"), lax.axis_index("pix")
    z, y = b // LINES, b % LINES
    other = 1 - y
    has_up, has_down = z < depth - 1, z > 0
    target = {UP: b + LINES, DOWN: b - LINES, ACROSS: z * LINES + other}
    allowed = {UP: has_up, DOWN: has_down}

    tpl_copy = pltpu.make_async_copy(tpl_hbm, tpl, local_sem.at[0])
    tpl_copy.start()

    names = routes_ref[...].astype(jnp.float32) + 1.0
    logs = jnp.log(iw_ref[...])
    infos[b] = jnp.zeros(infos.shape[1:], jnp.float32)
    for k in range(blocks):
        window = slice(k * rows, (k + 1) * rows)
        infos[b, 0:admits, window] = jnp.where(b == k, names, 0.0)
        infos[b, admits:admits + 1, window] = jnp.where(b == k, logs, 0.0)

    barrier = pltpu.get_barrier_semaphore()
    for way in (UP, DOWN):
        @pl.when(allowed[way])
        def _():
            pl.semaphore_signal(barrier, inc=1, device_id={"blk": target[way]}, device_id_type=MESH)
    pl.semaphore_signal(barrier, inc=1, device_id={"blk": target[ACROSS]}, device_id_type=MESH)
    for j in range(1, pixes):
        pl.semaphore_signal(barrier, inc=1, device_id={"pix": lax.rem(p + j, pixes)}, device_id_type=MESH)
    near = jnp.where(has_up, 1, 0) + jnp.where(has_down, 1, 0) + pixes
    pl.semaphore_wait(barrier, near)

    def cols(c):
        return pl.ds(c * width, width)

    def piece(way, k, c, own=False):
        return pltpu.make_async_remote_copy(
            src_ref=img_hbm.at[:, cols(c)] if own else buf.at[c, k],
            dst_ref=buf.at[c, k],
            send_sem=send_sem.at[way, k], recv_sem=recv_sem.at[k, c],
            device_id={"blk": target[way]}, device_id_type=MESH)

    def info_piece(way, k):
        return pltpu.make_async_remote_copy(
            src_ref=infos.at[k], dst_ref=infos.at[k],
            send_sem=info_send.at[way, k], recv_sem=info_recv.at[k],
            device_id={"blk": target[way]}, device_id_type=MESH)

    def arrived(k, c):
        pltpu.make_async_copy(buf.at[c, k], buf.at[c, k], recv_sem.at[k, c]).wait()

    def info_arrived(k):
        pltpu.make_async_copy(infos.at[k], infos.at[k], info_recv.at[k]).wait()

    def along(way, start):
        @pl.when(allowed[way])
        def _():
            start()

    for c in range(CHUNKS):
        piece(ACROSS, b, c, True).start()
        for way in (UP, DOWN):
            along(way, lambda: piece(way, b, c, True).start())
    for c in range(CHUNKS):
        pltpu.make_async_copy(img_hbm.at[:, cols(c)], buf.at[c, b], local_sem.at[1]).start()
    info_piece(ACROSS, b).start()
    for way in (UP, DOWN):
        along(way, lambda: info_piece(way, b).start())
    mate = z * LINES + other
    arrived(mate, 0)
    for way in (UP, DOWN):
        along(way, lambda: piece(way, mate, 0).start())

    def sides(d):
        return ((UP, z - d, z >= d), (DOWN, z + d, z + d < depth))

    def pass_on(d, c):
        for way, from_z, there in sides(d):
            k = from_z * LINES + y

            @pl.when(there)
            def _():
                arrived(k, c)
                if c:
                    piece(ACROSS, k, c).start()
                along(way, lambda: piece(way, k, c).start())

    def pass_rest(d):
        for way, from_z, there in sides(d):
            k, k2 = from_z * LINES + y, from_z * LINES + other

            @pl.when(there)
            def _():
                arrived(k2, 0)
                along(way, lambda: piece(way, k2, 0).start())
                info_arrived(k)
                info_piece(ACROSS, k).start()
                along(way, lambda: info_piece(way, k).start())

    half_z = depth // 2
    half = blocks // 2
    h = z // half_z

    def crossed(c, early):
        if c:
            if early:
                arrived(mate, c)
            for d in range(1, half_z if early else depth):
                for way, from_z, there in sides(d):
                    same = (from_z >= h * half_z) & (from_z < (h + 1) * half_z)

                    @pl.when(there & (same if early else jnp.logical_not(same)))
                    def _():
                        arrived(from_z * LINES + other, c)

    def product(c, side, fresh):
        images = buf[c, pl.ds(side * half, half)].reshape(half * rows, width)
        term = lax.dot_general(tpl[:, c * width:(c + 1) * width], images, (((1,), (1,)), ((), ())),
                               preferred_element_type=jnp.float32)
        if fresh:
            acc[side, 0:tpl_dev, :] = term
        else:
            acc[side, 0:tpl_dev, :] += term

    def my_part(e, j):
        return pltpu.make_async_remote_copy(
            src_ref=acc.at[h if e == 0 else 1 - h, pl.ds(lax.rem(p + j, pixes) * share, share), :],
            dst_ref=parts.at[e, j - 1],
            send_sem=part_send.at[e, j - 1], recv_sem=part_recv.at[e, j - 1],
            device_id={"pix": lax.rem(p + j, pixes)}, device_id_type=MESH)

    for d in range(1, depth - 1):
        for c in range(CHUNKS):
            pass_on(d, c)
        pass_rest(d)
    pltpu.make_async_copy(buf.at[:, b], buf.at[:, b], local_sem.at[1]).wait()
    tpl_copy.wait()
    if share * pixes > tpl_dev:
        acc[:, tpl_dev:, :] = jnp.zeros((2, share * pixes - tpl_dev, half * rows), jnp.float32)
    for c in range(CHUNKS):
        crossed(c, True)
        product(c, h, c == 0)
    for j in range(1, pixes):
        my_part(0, j).start()
    for c in range(CHUNKS + LAG):
        if c < CHUNKS:
            pass_on(depth - 1, c)
        if c == CHUNKS - 1:
            pass_rest(depth - 1)
        if c == CHUNKS + LAG - 1:
            product(0, 1 - h, False)
        if c > LAG:
            crossed(c - LAG, False)
            product(c - LAG, 1 - h, c - LAG == 1)

    for j in range(1, pixes):
        my_part(1, j).start()
    for c in range(CHUNKS):
        pltpu.make_async_copy(buf.at[c], gath_hbm.at[:, :, cols(c)], local_sem.at[3]).start()

    info_arrived(mate)
    for d in range(1, depth):
        for way, from_z, there in sides(d):
            @pl.when(there)
            def _():
                info_arrived(from_z * LINES + other)
    info = jnp.sum(infos[...], axis=0)
    code = (b + 1).astype(jnp.float32)
    admitted = jnp.max(jnp.where(info[0:admits, :] == code, 1.0, 0.0), axis=0, keepdims=True)
    image_log = info[admits:admits + 1, :]
    first = p * share
    here = (lax.broadcasted_iota(jnp.int32, (share, tpl_dev), 0) + first
            == lax.broadcasted_iota(jnp.int32, (share, tpl_dev), 1))
    template_log = jnp.sum(jnp.where(here, jnp.log(tw_ref[...].reshape(1, tpl_dev)), 0.0), axis=1, keepdims=True)
    valid = first + lax.broadcasted_iota(jnp.int32, (share, 1), 0) < tpl_dev
    sums = []
    for e, side in ((0, h), (1, 1 - h)):
        total = acc[side, pl.ds(pl.multiple_of(first, 16), share), :]
        for j in range(1, pixes):
            my_part(e, j).wait_recv()
            total = total + parts[e, j - 1]
        sums.append(total)
    scores = jnp.concatenate([jnp.where(h == 0, sums[0], sums[1]), jnp.where(h == 0, sums[1], sums[0])], axis=1)
    scores = jnp.where(admitted > 0, scores, NEG)

    me = b * pixes + p
    devices = blocks * pixes
    duals = jnp.zeros((1, blocks * rows), jnp.float32)
    for sweep in range(SWEEPS):
        terms = scores + duals
        peak = jnp.max(terms, axis=1, keepdims=True)
        level = template_log - peak - jnp.log(jnp.sum(jnp.exp(terms - peak), axis=1, keepdims=True))
        level = jnp.where(valid, level, NEG)
        terms = scores + level
        peak = jnp.max(terms, axis=0, keepdims=True)
        lse = peak + jnp.log(jnp.sum(jnp.exp(terms - peak), axis=0, keepdims=True))
        lse_out[sweep] = lse

        def post(j, carry):
            to = lax.rem(me + j, devices)
            pltpu.make_async_remote_copy(
                src_ref=lse_out.at[sweep], dst_ref=lse_in.at[sweep, me],
                send_sem=lse_send.at[sweep], recv_sem=lse_recv.at[sweep],
                device_id={"blk": to // pixes, "pix": lax.rem(to, pixes)}, device_id_type=MESH).start()
            return carry

        lax.fori_loop(1, devices, post, 0)
        lse_in[sweep, me] = lse
        span = lse_in.at[sweep, pl.ds(0, devices - 1)]
        pltpu.make_async_copy(span, span, lse_recv.at[sweep]).wait()
        every = lse_in[sweep]
        peak = jnp.max(every, axis=0)
        duals = image_log - peak - jnp.log(jnp.sum(jnp.exp(every - peak), axis=0))
    mine_only = jnp.zeros((1, rows), jnp.float32)
    for k in range(blocks):
        mine_only = jnp.where(b == k, duals[:, k * rows:(k + 1) * rows], mine_only)
    dual_ref[...] = mine_only
    terms = scores + duals
    weight = jnp.exp(terms - jnp.max(terms, axis=1, keepdims=True))
    mine = pl.ds(pl.multiple_of(first, 16), share)
    plan_ref[mine, :] = (weight / jnp.sum(weight, axis=1, keepdims=True)).astype(jnp.bfloat16)

    def my_plan(j):
        return pltpu.make_async_remote_copy(
            src_ref=plan_ref.at[mine, :], dst_ref=plan_ref.at[mine, :],
            send_sem=plan_send.at[j - 1], recv_sem=plan_recv.at[j - 1],
            device_id={"pix": lax.rem(p + j, pixes)}, device_id_type=MESH)

    for j in range(1, pixes):
        my_plan(j).start()

    full = buf.at[:, b]
    rest = buf.at[pl.ds(1, CHUNKS - 1), b]
    one = buf.at[0, b]

    def left(ref, sem):
        pltpu.make_async_copy(ref, ref, sem).wait()

    left(full, send_sem.at[ACROSS, b])
    left(infos.at[b], info_send.at[ACROSS, b])
    for way in (UP, DOWN):
        along(way, lambda: (left(full, send_sem.at[way, b]), left(one, send_sem.at[way, mate]),
                            left(infos.at[b], info_send.at[way, b])) and None)
    for d in range(1, depth):
        for way, from_z, there in sides(d):
            k, k2 = from_z * LINES + y, from_z * LINES + other

            @pl.when(there)
            def _():
                left(rest, send_sem.at[ACROSS, k])
                left(infos.at[b], info_send.at[ACROSS, k])
                along(way, lambda: (left(full, send_sem.at[way, k]), left(one, send_sem.at[way, k2]),
                                    left(infos.at[b], info_send.at[way, k])) and None)
    for j in range(1, pixes):
        my_part(0, j).wait_send()
        my_part(1, j).wait_send()
    for sweep in range(SWEEPS):
        span = lse_in.at[sweep, pl.ds(0, devices - 1)]
        left(span, lse_send.at[sweep])
    left(buf, local_sem.at[3])
    for j in range(1, pixes):
        my_plan(j).wait_send()
        my_plan(j).wait_recv()


def gathered(images, templates, routes, image_weight, template_weight):
    blocks, pixes = lax.axis_size("blk"), lax.axis_size("pix")
    rows, pixels = images.shape
    tpl_dev, admits = templates.shape[0], routes.shape[1]
    share = -(-tpl_dev // (16 * pixes)) * 16
    deep = -(-(admits + 1) // 8) * 8
    width = pixels // CHUNKS
    dims = (blocks, pixes, admits, tpl_dev, share)
    any_spec, vmem = pl.BlockSpec(memory_space=pl.ANY), pl.BlockSpec(memory_space=pltpu.VMEM)
    dma = pltpu.SemaphoreType.DMA
    devices = blocks * pixes
    gath, plan, duals = pl.pallas_call(
        functools.partial(gather_and_plan, dims),
        out_shape=(jax.ShapeDtypeStruct((blocks, rows, pixels), images.dtype),
                   jax.ShapeDtypeStruct((share * pixes, blocks * rows), jnp.bfloat16),
                   jax.ShapeDtypeStruct((1, rows), jnp.float32)),
        in_specs=[any_spec, any_spec, vmem, vmem, vmem],
        out_specs=(any_spec, vmem, vmem),
        scratch_shapes=[
            pltpu.VMEM((CHUNKS, blocks, rows, width), images.dtype),
            pltpu.VMEM((blocks, deep, blocks * rows), jnp.float32),
            pltpu.VMEM((tpl_dev, pixels), templates.dtype),
            pltpu.VMEM((2, share * pixes, blocks * rows // 2), jnp.float32),
            pltpu.VMEM((2, pixes - 1, share, blocks * rows // 2), jnp.float32),
            pltpu.VMEM((SWEEPS, 1, blocks * rows), jnp.float32),
            pltpu.VMEM((SWEEPS, devices, 1, blocks * rows), jnp.float32),
            dma((3, blocks)), dma((blocks, CHUNKS)), dma((3, blocks)), dma((blocks,)), dma((4,)),
            dma((2, pixes - 1)), dma((2, pixes - 1)), dma((SWEEPS,)), dma((SWEEPS,)),
            dma((pixes - 1,)), dma((pixes - 1,)),
        ],
        compiler_params=pltpu.CompilerParams(collective_id=0, has_side_effects=True),
    )(images, templates, routes.T, image_weight[None, :], template_weight)
    means = jnp.einsum("ti,ip->tp", plan[:tpl_dev], gath.reshape(blocks * rows, pixels),
                       preferred_element_type=jnp.float32).astype(jnp.bfloat16)
    return means, duals.reshape(-1)


def on_device(images, templates, routes, image_weight, template_weight):
    blocks = lax.axis_size("blk")
    if blocks * images.shape[0] <= templates.shape[0] and blocks % (2 * LINES) == 0:
        return gathered(images, templates, routes, image_weight, template_weight)
    return routed(images, templates, routes, image_weight, template_weight)


def solution(mesh):
    in_specs = (P("blk", "pix"), P("blk", "pix"), P("blk", None), P("blk"), P("blk"))
    out_specs = (P("blk", "pix"), P("blk"))
    return jax.shard_map(
        on_device, mesh=mesh, in_specs=in_specs, out_specs=out_specs, check_vma=False
    )
```

```python
import functools
import jax
import jax.numpy as jnp
from jax import lax
from jax.experimental import pallas as pl
from jax.experimental.pallas import tpu as pltpu
from jax.sharding import PartitionSpec as P

SWEEPS = 2
LINES = 2
CHUNKS = 4
LAG = 2
NEG = -1e30
MESH = pl.DeviceIdType.MESH
UP, DOWN, ACROSS = 0, 1, 2


def routed(images, templates, routes, image_weight, template_weight):
    blocks = lax.axis_size("blk")
    img_dev = images.shape[0]
    admits = routes.shape[1]
    capacity = max(2, (3 * img_dev * admits + 2 * blocks - 1) // (2 * blocks))
    target = routes.reshape(-1)
    target_hot = (target[:, None] == jnp.arange(blocks, dtype=jnp.int32)[None, :]).astype(jnp.int32)
    before = jnp.cumsum(target_hot, axis=0) - target_hot
    position = jnp.sum(before * target_hot, axis=1)
    slot_of = target * capacity + position
    wanted = jnp.arange(blocks * capacity, dtype=jnp.int32)
    matches = slot_of[None, :] == wanted[:, None]
    filled = jnp.any(matches, axis=1)
    owner_image = jnp.sum(
        jnp.where(matches, jnp.arange(target.shape[0], dtype=jnp.int32)[None, :] // admits, 0),
        axis=1,
    )
    outgoing = jnp.where(filled[:, None], images[owner_image], jnp.zeros((), images.dtype))
    outgoing = outgoing.reshape(blocks, capacity, images.shape[1])
    slot_flags = filled.astype(jnp.bfloat16).reshape(blocks, capacity)
    template_log = jnp.log(template_weight)
    arrived_piece = lax.all_to_all(outgoing, "blk", split_axis=0, concat_axis=0, tiled=True)
    marks_piece = lax.all_to_all(slot_flags, "blk", split_axis=0, concat_axis=0, tiled=True)
    partial_value = jnp.einsum(
        "bmp,tp->bmt", arrived_piece, templates, preferred_element_type=jnp.float32
    )
    summed = lax.psum(partial_value, "pix")
    usable = marks_piece > 0
    image_log = jnp.log(image_weight)
    slot_duals = jnp.zeros((blocks, capacity), jnp.float32)
    image_duals = jnp.zeros((img_dev,), jnp.float32)
    for sweep_index in range(SWEEPS):
        column_terms = jnp.where(usable[:, :, None], summed + slot_duals[:, :, None], -jnp.inf)
        column_peak = jnp.max(column_terms, axis=(0, 1))
        template_duals = (
            template_log
            - column_peak
            - jnp.log(jnp.sum(jnp.exp(column_terms - column_peak), axis=(0, 1)))
        )
        row_terms = summed + template_duals
        row_peak = jnp.max(row_terms, axis=2)
        row_total = jnp.sum(jnp.exp(row_terms - row_peak[:, :, None]), axis=2)
        levels = row_peak + jnp.log(row_total)
        back_levels = lax.all_to_all(levels, "blk", split_axis=0, concat_axis=0, tiled=True)
        level_routes = back_levels.reshape(-1)[slot_of].reshape(img_dev, admits)
        route_peak = jnp.max(level_routes, axis=1)
        image_duals = (
            image_log
            - route_peak
            - jnp.log(jnp.sum(jnp.exp(level_routes - route_peak[:, None]), axis=1))
        )
        duals_send = jnp.where(filled, image_duals[owner_image], 0.0).reshape(blocks, capacity)
        slot_duals = lax.all_to_all(duals_send, "blk", split_axis=0, concat_axis=0, tiled=True)
    column_terms = jnp.where(usable[:, :, None], summed + slot_duals[:, :, None], -jnp.inf)
    column_peak = jnp.max(column_terms, axis=(0, 1))
    column_exp = jnp.exp(column_terms - column_peak)
    plan_weights = (column_exp / jnp.sum(column_exp, axis=(0, 1))).astype(jnp.bfloat16)
    template_means = jnp.einsum(
        "bmt,bmp->tp", plan_weights, arrived_piece, preferred_element_type=jnp.float32
    ).astype(jnp.bfloat16)
    return (template_means, image_duals)


def gather_and_plan(dims, img_hbm, tpl_hbm, routes_ref, iw_ref, tw_ref, gath_hbm, plan_ref, dual_ref,
                    buf, infos, tpl, acc, parts, lse_out, lse_in,
                    send_sem, recv_sem, info_send, info_recv, local_sem,
                    part_send, part_recv, lse_send, lse_recv, plan_send, plan_recv):
    blocks, pixes, admits, tpl_dev, share = dims
    depth = blocks // LINES
    rows, pixels = img_hbm.shape
    width = pixels // CHUNKS
    b, p = lax.axis_index("blk"), lax.axis_index("pix")
    z, y = b // LINES, b % LINES
    other = 1 - y
    has_up, has_down = z < depth - 1, z > 0
    target = {UP: b + LINES, DOWN: b - LINES, ACROSS: z * LINES + other}
    allowed = {UP: has_up, DOWN: has_down}

    tpl_copy = pltpu.make_async_copy(tpl_hbm, tpl, local_sem.at[0])
    tpl_copy.start()

    names = routes_ref[...].astype(jnp.float32) + 1.0
    logs = jnp.log(iw_ref[...])
    infos[b] = jnp.zeros(infos.shape[1:], jnp.float32)
    for k in range(blocks):
        window = slice(k * rows, (k + 1) * rows)
        infos[b, 0:admits, window] = jnp.where(b == k, names, 0.0)
        infos[b, admits:admits + 1, window] = jnp.where(b == k, logs, 0.0)

    barrier = pltpu.get_barrier_semaphore()
    for way in (UP, DOWN):
        @pl.when(allowed[way])
        def _():
            pl.semaphore_signal(barrier, inc=1, device_id={"blk": target[way]}, device_id_type=MESH)
    pl.semaphore_signal(barrier, inc=1, device_id={"blk": target[ACROSS]}, device_id_type=MESH)
    for j in range(1, pixes):
        pl.semaphore_signal(barrier, inc=1, device_id={"pix": lax.rem(p + j, pixes)}, device_id_type=MESH)
    near = jnp.where(has_up, 1, 0) + jnp.where(has_down, 1, 0) + pixes
    pl.semaphore_wait(barrier, near)

    def cols(c):
        return pl.ds(c * width, width)

    def piece(way, k, c, own=False):
        return pltpu.make_async_remote_copy(
            src_ref=img_hbm.at[:, cols(c)] if own else buf.at[c, k],
            dst_ref=buf.at[c, k],
            send_sem=send_sem.at[way, k], recv_sem=recv_sem.at[k, c],
            device_id={"blk": target[way]}, device_id_type=MESH)

    def info_piece(way, k):
        return pltpu.make_async_remote_copy(
            src_ref=infos.at[k], dst_ref=infos.at[k],
            send_sem=info_send.at[way, k], recv_sem=info_recv.at[k],
            device_id={"blk": target[way]}, device_id_type=MESH)

    def arrived(k, c):
        pltpu.make_async_copy(buf.at[c, k], buf.at[c, k], recv_sem.at[k, c]).wait()

    def info_arrived(k):
        pltpu.make_async_copy(infos.at[k], infos.at[k], info_recv.at[k]).wait()

    def along(way, start):
        @pl.when(allowed[way])
        def _():
            start()

    for c in range(CHUNKS):
        piece(ACROSS, b, c, True).start()
        for way in (UP, DOWN):
            along(way, lambda: piece(way, b, c, True).start())
    for c in range(CHUNKS):
        pltpu.make_async_copy(img_hbm.at[:, cols(c)], buf.at[c, b], local_sem.at[1]).start()
    info_piece(ACROSS, b).start()
    for way in (UP, DOWN):
        along(way, lambda: info_piece(way, b).start())
    mate = z * LINES + other
    arrived(mate, 0)
    for way in (UP, DOWN):
        along(way, lambda: piece(way, mate, 0).start())

    def sides(d):
        return ((UP, z - d, z >= d), (DOWN, z + d, z + d < depth))

    def pass_on(d, c):
        for way, from_z, there in sides(d):
            k = from_z * LINES + y

            @pl.when(there)
            def _():
                arrived(k, c)
                if c:
                    piece(ACROSS, k, c).start()
                along(way, lambda: piece(way, k, c).start())

    def pass_rest(d):
        for way, from_z, there in sides(d):
            k, k2 = from_z * LINES + y, from_z * LINES + other

            @pl.when(there)
            def _():
                arrived(k2, 0)
                along(way, lambda: piece(way, k2, 0).start())
                info_arrived(k)
                info_piece(ACROSS, k).start()
                along(way, lambda: info_piece(way, k).start())

    half_z = depth // 2
    half = blocks // 2
    h = z // half_z

    def crossed(c, early):
        if c:
            if early:
                arrived(mate, c)
            for d in range(1, half_z if early else depth):
                for way, from_z, there in sides(d):
                    same = (from_z >= h * half_z) & (from_z < (h + 1) * half_z)

                    @pl.when(there & (same if early else jnp.logical_not(same)))
                    def _():
                        arrived(from_z * LINES + other, c)

    def product(c, side, fresh):
        images = buf[c, pl.ds(side * half, half)].reshape(half * rows, width)
        term = lax.dot_general(tpl[:, c * width:(c + 1) * width], images, (((1,), (1,)), ((), ())),
                               preferred_element_type=jnp.float32)
        if fresh:
            acc[side, 0:tpl_dev, :] = term
        else:
            acc[side, 0:tpl_dev, :] += term

    def my_part(e, j):
        return pltpu.make_async_remote_copy(
            src_ref=acc.at[h if e == 0 else 1 - h, pl.ds(lax.rem(p + j, pixes) * share, share), :],
            dst_ref=parts.at[e, j - 1],
            send_sem=part_send.at[e, j - 1], recv_sem=part_recv.at[e, j - 1],
            device_id={"pix": lax.rem(p + j, pixes)}, device_id_type=MESH)

    for d in range(1, depth - 1):
        for c in range(CHUNKS):
            pass_on(d, c)
        pass_rest(d)
    pltpu.make_async_copy(buf.at[:, b], buf.at[:, b], local_sem.at[1]).wait()
    tpl_copy.wait()
    if share * pixes > tpl_dev:
        acc[:, tpl_dev:, :] = jnp.zeros((2, share * pixes - tpl_dev, half * rows), jnp.float32)
    for c in range(CHUNKS):
        crossed(c, True)
        product(c, h, c == 0)
    for j in range(1, pixes):
        my_part(0, j).start()
    for c in range(CHUNKS + LAG):
        if c < CHUNKS:
            pass_on(depth - 1, c)
        if c == CHUNKS - 1:
            pass_rest(depth - 1)
        if c == CHUNKS + LAG - 1:
            product(0, 1 - h, False)
        if c > LAG:
            crossed(c - LAG, False)
            product(c - LAG, 1 - h, c - LAG == 1)

    for j in range(1, pixes):
        my_part(1, j).start()
    for c in range(CHUNKS):
        pltpu.make_async_copy(buf.at[c], gath_hbm.at[:, :, cols(c)], local_sem.at[3]).start()

    info_arrived(mate)
    for d in range(1, depth):
        for way, from_z, there in sides(d):
            @pl.when(there)
            def _():
                info_arrived(from_z * LINES + other)
    info = jnp.sum(infos[...], axis=0)
    code = (b + 1).astype(jnp.float32)
    admitted = jnp.max(jnp.where(info[0:admits, :] == code, 1.0, 0.0), axis=0, keepdims=True)
    image_log = info[admits:admits + 1, :]
    first = p * share
    here = (lax.broadcasted_iota(jnp.int32, (share, tpl_dev), 0) + first
            == lax.broadcasted_iota(jnp.int32, (share, tpl_dev), 1))
    template_log = jnp.sum(jnp.where(here, jnp.log(tw_ref[...].reshape(1, tpl_dev)), 0.0), axis=1, keepdims=True)
    valid = first + lax.broadcasted_iota(jnp.int32, (share, 1), 0) < tpl_dev
    sums = []
    for e, side in ((0, h), (1, 1 - h)):
        total = acc[side, pl.ds(pl.multiple_of(first, 16), share), :]
        for j in range(1, pixes):
            my_part(e, j).wait_recv()
            total = total + parts[e, j - 1]
        sums.append(total)
    scores = jnp.concatenate([jnp.where(h == 0, sums[0], sums[1]), jnp.where(h == 0, sums[1], sums[0])], axis=1)
    scores = jnp.where(admitted > 0, scores, NEG)

    me = b * pixes + p
    devices = blocks * pixes
    duals = jnp.zeros((1, blocks * rows), jnp.float32)
    for sweep in range(SWEEPS):
        terms = scores + duals
        peak = jnp.max(terms, axis=1, keepdims=True)
        level = template_log - peak - jnp.log(jnp.sum(jnp.exp(terms - peak), axis=1, keepdims=True))
        level = jnp.where(valid, level, NEG)
        terms = scores + level
        peak = jnp.max(terms, axis=0, keepdims=True)
        lse = peak + jnp.log(jnp.sum(jnp.exp(terms - peak), axis=0, keepdims=True))
        lse_out[sweep] = lse

        def post(j, carry):
            to = lax.rem(me + j, devices)
            pltpu.make_async_remote_copy(
                src_ref=lse_out.at[sweep], dst_ref=lse_in.at[sweep, me],
                send_sem=lse_send.at[sweep], recv_sem=lse_recv.at[sweep],
                device_id={"blk": to // pixes, "pix": lax.rem(to, pixes)}, device_id_type=MESH).start()
            return carry

        lax.fori_loop(1, devices, post, 0)
        lse_in[sweep, me] = lse
        span = lse_in.at[sweep, pl.ds(0, devices - 1)]
        pltpu.make_async_copy(span, span, lse_recv.at[sweep]).wait()
        every = lse_in[sweep]
        peak = jnp.max(every, axis=0)
        duals = image_log - peak - jnp.log(jnp.sum(jnp.exp(every - peak), axis=0))
    mine_only = jnp.zeros((1, rows), jnp.float32)
    for k in range(blocks):
        mine_only = jnp.where(b == k, duals[:, k * rows:(k + 1) * rows], mine_only)
    dual_ref[...] = mine_only
    terms = scores + duals
    weight = jnp.exp(terms - jnp.max(terms, axis=1, keepdims=True))
    mine = pl.ds(pl.multiple_of(first, 16), share)
    plan_ref[mine, :] = (weight / jnp.sum(weight, axis=1, keepdims=True)).astype(jnp.bfloat16)

    def my_plan(j):
        return pltpu.make_async_remote_copy(
            src_ref=plan_ref.at[mine, :], dst_ref=plan_ref.at[mine, :],
            send_sem=plan_send.at[j - 1], recv_sem=plan_recv.at[j - 1],
            device_id={"pix": lax.rem(p + j, pixes)}, device_id_type=MESH)

    for j in range(1, pixes):
        my_plan(j).start()

    full = buf.at[:, b]
    rest = buf.at[pl.ds(1, CHUNKS - 1), b]
    one = buf.at[0, b]

    def left(ref, sem):
        pltpu.make_async_copy(ref, ref, sem).wait()

    left(full, send_sem.at[ACROSS, b])
    left(infos.at[b], info_send.at[ACROSS, b])
    for way in (UP, DOWN):
        along(way, lambda: (left(full, send_sem.at[way, b]), left(one, send_sem.at[way, mate]),
                            left(infos.at[b], info_send.at[way, b])) and None)
    for d in range(1, depth):
        for way, from_z, there in sides(d):
            k, k2 = from_z * LINES + y, from_z * LINES + other

            @pl.when(there)
            def _():
                left(rest, send_sem.at[ACROSS, k])
                left(infos.at[b], info_send.at[ACROSS, k])
                along(way, lambda: (left(full, send_sem.at[way, k]), left(one, send_sem.at[way, k2]),
                                    left(infos.at[b], info_send.at[way, k])) and None)
    for j in range(1, pixes):
        my_part(0, j).wait_send()
        my_part(1, j).wait_send()
    for sweep in range(SWEEPS):
        span = lse_in.at[sweep, pl.ds(0, devices - 1)]
        left(span, lse_send.at[sweep])
    left(buf, local_sem.at[3])
    for j in range(1, pixes):
        my_plan(j).wait_send()
        my_plan(j).wait_recv()


def gathered(images, templates, routes, image_weight, template_weight):
    blocks, pixes = lax.axis_size("blk"), lax.axis_size("pix")
    rows, pixels = images.shape
    tpl_dev, admits = templates.shape[0], routes.shape[1]
    share = -(-tpl_dev // (16 * pixes)) * 16
    deep = -(-(admits + 1) // 8) * 8
    width = pixels // CHUNKS
    dims = (blocks, pixes, admits, tpl_dev, share)
    any_spec, vmem = pl.BlockSpec(memory_space=pl.ANY), pl.BlockSpec(memory_space=pltpu.VMEM)
    dma = pltpu.SemaphoreType.DMA
    devices = blocks * pixes
    gath, plan, duals = pl.pallas_call(
        functools.partial(gather_and_plan, dims),
        out_shape=(jax.ShapeDtypeStruct((blocks, rows, pixels), images.dtype),
                   jax.ShapeDtypeStruct((share * pixes, blocks * rows), jnp.bfloat16),
                   jax.ShapeDtypeStruct((1, rows), jnp.float32)),
        in_specs=[any_spec, any_spec, vmem, vmem, vmem],
        out_specs=(any_spec, vmem, vmem),
        scratch_shapes=[
            pltpu.VMEM((CHUNKS, blocks, rows, width), images.dtype),
            pltpu.VMEM((blocks, deep, blocks * rows), jnp.float32),
            pltpu.VMEM((tpl_dev, pixels), templates.dtype),
            pltpu.VMEM((2, share * pixes, blocks * rows // 2), jnp.float32),
            pltpu.VMEM((2, pixes - 1, share, blocks * rows // 2), jnp.float32),
            pltpu.VMEM((SWEEPS, 1, blocks * rows), jnp.float32),
            pltpu.VMEM((SWEEPS, devices, 1, blocks * rows), jnp.float32),
            dma((3, blocks)), dma((blocks, CHUNKS)), dma((3, blocks)), dma((blocks,)), dma((4,)),
            dma((2, pixes - 1)), dma((2, pixes - 1)), dma((SWEEPS,)), dma((SWEEPS,)),
            dma((pixes - 1,)), dma((pixes - 1,)),
        ],
        compiler_params=pltpu.CompilerParams(collective_id=0, has_side_effects=True),
    )(images, templates, routes.T, image_weight[None, :], template_weight)
    means = jnp.einsum("ti,ip->tp", plan[:tpl_dev], gath.reshape(blocks * rows, pixels),
                       preferred_element_type=jnp.float32).astype(jnp.bfloat16)
    return means, duals.reshape(-1)


def on_device(images, templates, routes, image_weight, template_weight):
    blocks = lax.axis_size("blk")
    if blocks * images.shape[0] <= templates.shape[0] and blocks % (2 * LINES) == 0:
        return gathered(images, templates, routes, image_weight, template_weight)
    return routed(images, templates, routes, image_weight, template_weight)


def solution(mesh):
    in_specs = (P("blk", "pix"), P("blk", "pix"), P("blk", None), P("blk"), P("blk"))
    out_specs = (P("blk", "pix"), P("blk"))
    return jax.shard_map(
        on_device, mesh=mesh, in_specs=in_specs, out_specs=out_specs, check_vma=False
    )
```
